256 devices in a mesh: inb: 16 (over x, y), outb: 16 (over z, core).
Axes of the slice: x: 4, y: 4, z: 8, core: 2. Of those that a mesh axis runs over, the one named last changes fastest.
Arguments:
- tokens: bfloat16 [512, 8192], P('outb', 'inb'), may hold values from -6 to 6
- grad_out: bfloat16 [512, 8192], P('outb', 'inb'), may hold values from -6 to 6
- gate_weight: bfloat16 [8192, 28672], P('inb', 'outb'), may hold values from -0.09375 to 0.09375
- up_weight: bfloat16 [8192, 28672], P('inb', 'outb'), may hold values from -0.09375 to 0.09375
- down_weight: bfloat16 [28672, 8192], P('outb', 'inb'), may hold values from -0.046875 to 0.046875
- gate_mask: int32 [64, 224], P('inb', 'outb'), may hold values 0 or 1
- up_mask: int32 [64, 224], P('inb', 'outb'), may hold values 0 or 1
- down_mask: int32 [224, 64], P('outb', 'inb'), may hold values 0 or 1
Outputs:
- layer_out: bfloat16 [512, 8192], P('outb', 'inb')
- grad_tokens: bfloat16 [512, 8192], P('outb', 'inb')
- grad_gate: bfloat16 [8192, 28672], P('inb', 'outb')
- grad_up: bfloat16 [8192, 28672], P('inb', 'outb')
- grad_down: bfloat16 [28672, 8192], P('outb', 'inb')
The draws below stay inside these ranges and needn't reach their ends.
All inputs are finite; a program needn't handle non-finite values. No bound on the sum of `gate_mask` or of `up_mask` or of `down_mask` on one device may be relied on, other than what follows from the above.
Results may differ from the reference program's by a relative error of at most 0.0049.
Values may be sent and summed in bfloat16 or wider, within the bound.
A program may use at most 128 MiB of HBM per device.

```python
import jax
import jax.numpy as jnp

D = 8192
FF = 28672
BLOCK = 128
TOKENS = 512


def plant(values, own_key, least, top_value):
    spot = [jax.random.randint(jax.random.fold_in(own_key, axis), (), 0, length) for axis, length in enumerate(values.shape)]
    main_axis = values.shape.index(max(values.shape))
    neighbour = spot[:main_axis] + [(spot[main_axis] + 1) % values.shape[main_axis]] + spot[main_axis + 1:]
    return values.at[tuple(spot)].set(least).at[tuple(neighbour)].set(top_value)


def levels(rng, shape, pieces, least, high):
    factor_of = 1.0
    for position, blocks in pieces:
        heights = jax.random.uniform(jax.random.fold_in(jax.random.fold_in(rng, 6), position), (blocks,), jnp.float32, least / len(pieces), high / len(pieces))
        factor_of = factor_of * jnp.repeat(jnp.exp(heights), shape[position] // blocks).reshape((-1,) + (1,) * (len(shape) - 1 - position))
    return factor_of


def centred(own_key, dims, width, limit, shards=(), kind=jnp.bfloat16):
    values = width * jax.random.normal(own_key, dims, jnp.float32)
    if shards:
        values = values * levels(own_key, dims, shards, -0.22, 0.18)
    return jnp.clip(values, -limit, limit).astype(kind)


def setup_inputs(seed: int = 0) -> dict:
    streams_of = jax.random.split(jax.random.key(seed), 9)
    tokens = centred(streams_of[0], (TOKENS, D), 1.0, 6.0, ((0, 16), (1, 16)))
    grad_out = centred(streams_of[1], (TOKENS, D), 1.0, 6.0, ((0, 16), (1, 16)))
    gate_weight = centred(streams_of[2], (D, FF), (D // 2) ** -0.5, 0.09375, ((0, 16), (1, 16)))
    up_weight = centred(streams_of[3], (D, FF), (D // 2) ** -0.5, 0.09375, ((0, 16), (1, 16)))
    down_weight = centred(streams_of[4], (FF, D), (FF // 2) ** -0.5, 0.046875, ((0, 16), (1, 16)))
    gate_mask = plant((jax.random.randint(streams_of[5], (D // BLOCK, FF // BLOCK), 0, 2) < 1).astype(jnp.int32), jax.random.fold_in(streams_of[5], 1), 0, 1)
    up_mask = plant((jax.random.randint(streams_of[6], (D // BLOCK, FF // BLOCK), 0, 2) < 1).astype(jnp.int32), jax.random.fold_in(streams_of[6], 1), 0, 1)
    down_mask = plant((jax.random.randint(streams_of[7], (FF // BLOCK, D // BLOCK), 0, 2) < 1).astype(jnp.int32), jax.random.fold_in(streams_of[7], 1), 0, 1)
    return {"tokens": tokens, "grad_out": grad_out, "gate_weight": gate_weight, "up_weight": up_weight, "down_weight": down_weight, "gate_mask": gate_mask, "up_mask": up_mask, "down_mask": down_mask}


def expand(weight, mask):
    rows, cols = mask.shape
    blocks = weight.reshape(rows, BLOCK, cols, BLOCK)
    return (blocks * mask.astype(weight.dtype)[:, None, :, None]).reshape(weight.shape)


def reference(tokens, grad_out, gate_weight, up_weight, down_weight, gate_mask, up_mask, down_mask):
    gate_sparse = expand(gate_weight, gate_mask)
    up_sparse = expand(up_weight, up_mask)
    down_sparse = expand(down_weight, down_mask)
    gate = jnp.dot(tokens, gate_sparse, preferred_element_type=jnp.float32)
    up = jnp.dot(tokens, up_sparse, preferred_element_type=jnp.float32)
    sigmoid_gate = jax.nn.sigmoid(gate)
    hidden = (gate * sigmoid_gate * up).astype(jnp.bfloat16)
    layer_out = jnp.dot(hidden, down_sparse, preferred_element_type=jnp.float32).astype(jnp.bfloat16)
    hidden_grad = jnp.dot(grad_out, down_sparse.T, preferred_element_type=jnp.float32)
    gate_grad = (hidden_grad * up * sigmoid_gate * (1.0 + gate * (1.0 - sigmoid_gate))).astype(jnp.bfloat16)
    up_grad = (hidden_grad * gate * sigmoid_gate).astype(jnp.bfloat16)
    grad_tokens = (jnp.dot(gate_grad, gate_sparse.T, preferred_element_type=jnp.float32)
                   + jnp.dot(up_grad, up_sparse.T, preferred_element_type=jnp.float32)).astype(jnp.bfloat16)
    grad_gate = expand(jnp.dot(tokens.T, gate_grad, preferred_element_type=jnp.float32), gate_mask).astype(jnp.bfloat16)
    grad_up = expand(jnp.dot(tokens.T, up_grad, preferred_element_type=jnp.float32), up_mask).astype(jnp.bfloat16)
    grad_down = expand(jnp.dot(hidden.T, grad_out, preferred_element_type=jnp.float32), down_mask).astype(jnp.bfloat16)
    return layer_out, grad_tokens, grad_gate, grad_up, grad_down
```

```python
import functools

import jax
import jax.numpy as jnp
from jax import lax
from jax.experimental import pallas as pl
from jax.experimental.pallas import tpu as pltpu
from jax.sharding import PartitionSpec as P

MESH = pl.DeviceIdType.MESH
F32 = jnp.float32
BF16 = jnp.bfloat16
SIDE = 4
ZS = 8
GROUP = SIDE * SIDE
ROWS = 32
TOK = GROUP * ROWS
WID = 512
HID = 1792
LANES = 128
CH = 2 * LANES
NR = HID // CH
STAGES = 5


def dot(a, b):
    return jnp.dot(a, b, preferred_element_type=F32)


def dot_nt(a, b):
    return lax.dot_general(a, b, (((1,), (1,)), ((), ())), preferred_element_type=F32)


def dot_tn(a, b):
    return lax.dot_general(a, b, (((0,), (0,)), ((), ())), preferred_element_type=F32)


def kernel(
    tokens, grad_out, gate_w, up_w, down_w, gate_m, up_m, down_m,
    layer_out, grad_tokens, grad_gate, grad_up, grad_down,
    ab, tok_t, gw, uw, dw, part, own, recv1, mid, mid_own, recv2, full,
    out_g, out_u, out_d, acc, xbuf, zsend, zown, zrecv,
    load_sem, w_sem, a_send, a_recv, s_send, s_recv,
    send1, got1, send2, got2, send3, got3, send4, got4, out_sem,
    x_send, x_recv, z_send, z_recv,
):
    i = lax.axis_index("inb")
    o = lax.axis_index("outb")
    x, y = i // SIDE, lax.rem(i, SIDE)
    z, c = o // 2, lax.rem(o, 2)
    sib = 1 - c

    def at_x(k):
        return (lax.rem(x + k, SIDE) * SIDE + y, o)

    def at_y(k):
        return (x * SIDE + lax.rem(y + k, SIDE), o)

    def at_z(k):
        return (i, lax.rem(z + k, ZS) * 2 + c)

    sibling = (i, z * 2 + sib)

    def remote(src, dst, s, r, device):
        return pltpu.make_async_remote_copy(
            src_ref=src, dst_ref=dst, send_sem=s, recv_sem=r,
            device_id=device, device_id_type=MESH,
        )

    def drain(ref, sem):
        pltpu.make_async_copy(ref, ref, sem).wait()

    mine = c * ZS + z
    first = [
        pltpu.make_async_copy(tokens, ab.at[mine, 0], load_sem.at[0]),
        pltpu.make_async_copy(grad_out, ab.at[mine, 1], load_sem.at[1]),
    ]
    for copy in first:
        copy.start()
    weights = []
    for r in range(NR):
        cols = pl.ds(r * CH, CH)
        weights.append(pltpu.make_async_copy(gate_w.at[:, cols], gw.at[r], w_sem.at[0, r]))
        weights.append(pltpu.make_async_copy(up_w.at[:, cols], uw.at[r], w_sem.at[1, r]))
        weights.append(pltpu.make_async_copy(down_w.at[cols, :], dw.at[r], w_sem.at[2, r]))
    for copy in weights:
        copy.start()

    barrier = pltpu.get_barrier_semaphore()
    for k in range(1, SIDE):
        pl.semaphore_signal(barrier, inc=1, device_id=at_x(k), device_id_type=MESH)
        pl.semaphore_signal(barrier, inc=1, device_id=at_y(k), device_id_type=MESH)
    for k in range(1, ZS):
        pl.semaphore_signal(barrier, inc=1, device_id=at_z(k), device_id_type=MESH)
    pl.semaphore_signal(barrier, inc=1, device_id=sibling, device_id_type=MESH)
    pl.semaphore_wait(barrier, 2 * (SIDE - 1) + ZS - 1 + 1)

    for copy in first:
        copy.wait()
    own_block = ab.at[mine]
    order = (1, 7, 2, 6, 3, 5, 4)
    z_copies = [remote(own_block, own_block, a_send.at[k - 1], a_recv.at[k - 1], at_z(k)) for k in order]
    for copy in z_copies:
        copy.start()
    to_sib = [remote(own_block, own_block, s_send.at[0], s_recv, sibling)]
    to_sib[0].start()

    for copy in weights:
        copy.wait()
    for r in range(NR):
        for a in range(WID // LANES):
            for b in range(2):
                rows, cols = pl.ds(a * LANES, LANES), pl.ds(b * LANES, LANES)
                for w, m in ((gw, gate_m), (uw, up_m)):
                    keep = jnp.full((LANES, LANES), m[a, 2 * r + b].astype(F32), F32)
                    w[r, rows, cols] = w[r, rows, cols] * keep.astype(BF16)
                keep = jnp.full((LANES, LANES), down_m[2 * r + b, a].astype(F32), F32)
                dw[r, cols, rows] = dw[r, cols, rows] * keep.astype(BF16)

    for n, k in enumerate(order):
        block = ab.at[c * ZS + lax.rem(z + ZS - k, ZS)]
        remote(block, block, a_send.at[k - 1], a_recv.at[k - 1], at_z(k)).wait_recv()
        copy = remote(block, block, s_send.at[n + 1], s_recv, sibling)
        copy.start()
        to_sib.append(copy)
    drain(ab.at[pl.ds(sib * ZS, ZS)], s_recv)

    acc[...] = jnp.zeros_like(acc)

    def places(h):
        return (at_x, at_y, x, y) if h == 0 else (at_y, at_x, y, x)

    def partial_sums(r):
        tok = ab[:, 0].reshape(TOK, WID)
        cot = ab[:, 1].reshape(TOK, WID)
        slot = lax.rem(r, 2)
        for n in range(3):
            if n == 0:
                value = dot(tok, gw[r])
            elif n == 1:
                value = dot(tok, uw[r])
            else:
                value = dot_nt(cot, dw[r])
            for h in range(2):
                piece = value[:, h * LANES:(h + 1) * LANES].reshape(GROUP, ROWS, LANES)
                own[slot, h, :, n] = piece
                part[r, h, :, n] = piece.astype(BF16)
        for h in range(2):
            at1, _, p1, _ = places(h)
            for k in range(1, SIDE):
                to = lax.rem(p1 + k, SIDE)
                remote(
                    part.at[r, h, pl.ds(to * SIDE, SIDE)], recv1.at[r, h, k - 1],
                    send1.at[r, h], got1.at[r, h], at1(k),
                ).start()

    def second(r):
        slot = lax.rem(r, 2)
        for h in range(2):
            _, at2, p1, p2 = places(h)
            drain(recv1.at[r, h], got1.at[r, h])
            total = own[slot, h, pl.ds(p1 * SIDE, SIDE)]
            for k in range(SIDE - 1):
                total = total + recv1[r, h, k].astype(F32)
            mid_own[slot, h] = total
            mid[r, h] = total.astype(BF16)
            for k in range(1, SIDE):
                to = lax.rem(p2 + k, SIDE)
                remote(
                    mid.at[r, h, to], recv2.at[r, h, k - 1],
                    send2.at[r, h], got2.at[r, h], at2(k),
                ).start()

    def activations(r):
        slot = lax.rem(r, 2)
        for h in range(2):
            _, at2, p1, p2 = places(h)
            drain(recv2.at[r, h], got2.at[r, h])
            total = mid_own[slot, h, p2]
            for k in range(SIDE - 1):
                total = total + recv2[r, h, k].astype(F32)
            gate, up, hidden_grad = total[0], total[1], total[2]
            sig = jax.nn.sigmoid(gate)
            act = gate * sig
            at = p1 * SIDE + p2
            full[r, h, at, 0] = (act * up).astype(BF16)
            full[r, h, at, 1] = (hidden_grad * up * sig * (1.0 + gate * (1.0 - sig))).astype(BF16)
            full[r, h, at, 2] = (hidden_grad * act).astype(BF16)
            for k in range(1, SIDE):
                block = full.at[r, h, at]
                remote(block, block, send3.at[r, h], got3.at[r, h], at2(k)).start()

    def spread(r):
        for h in range(2):
            at1, _, p1, _ = places(h)
            drain(recv2.at[r, h], got3.at[r, h])
            for k in range(1, SIDE):
                block = full.at[r, h, pl.ds(p1 * SIDE, SIDE)]
                remote(block, block, send4.at[r, h], got4.at[r, h], at1(k)).start()

    def finish(r):
        drain(recv1.at[r, 0], got4.at[r, 0])
        drain(recv1.at[r, 1], got4.at[r, 1])

        def whole(n):
            return jnp.concatenate(
                [full[r, h, :, n].reshape(TOK, LANES) for h in range(2)], axis=1
            )

        hidden, gate_grad, up_grad = whole(0), whole(1), whole(2)
        half = TOK // 2
        value = dot(hidden, dw[r])
        acc[0, 0] += value[:half]
        acc[1, 0] += value[half:]
        value = dot_nt(gate_grad, gw[r]) + dot_nt(up_grad, uw[r])
        acc[0, 1] += value[:half]
        acc[1, 1] += value[half:]
        cot = ab[:, 1].reshape(TOK, WID)
        for out, left, m in ((out_g, gate_grad, gate_m), (out_u, up_grad, up_m)):
            value = dot(tok_t[...], left)
            for a in range(WID // LANES):
                for b in range(2):
                    rows, cols = slice(a * LANES, (a + 1) * LANES), slice(b * LANES, (b + 1) * LANES)
                    keep = m[a, 2 * r + b].astype(F32)
                    out[r, rows, cols] = (value[rows, cols] * keep).astype(BF16)
        value = dot_tn(hidden, cot)
        for a in range(WID // LANES):
            for b in range(2):
                rows, cols = slice(a * LANES, (a + 1) * LANES), slice(b * LANES, (b + 1) * LANES)
                keep = down_m[2 * r + b, a].astype(F32)
                out_d[r, cols, rows] = (value[cols, rows] * keep).astype(BF16)
        for copy in outs(r):
            copy.start()

    def outs(r):
        cols = pl.ds(pl.multiple_of(r * CH, CH), CH)
        return [
            pltpu.make_async_copy(out_g.at[r], grad_gate.at[:, cols], out_sem.at[0, r]),
            pltpu.make_async_copy(out_u.at[r], grad_up.at[:, cols], out_sem.at[1, r]),
            pltpu.make_async_copy(out_d.at[r], grad_down.at[cols, :], out_sem.at[2, r]),
        ]

    @pl.loop(0, NR + STAGES - 1)
    def _(t):
        for stage, work in enumerate((partial_sums, second, activations, spread, finish)):
            @pl.when(jnp.logical_and(t >= stage, t < NR + stage))
            def _():
                work(t - stage)

            if stage == 0:
                @pl.when(t == 1)
                def _():
                    tok_t[...] = ab[:, 0].reshape(TOK, WID).T

    copy = remote(acc.at[sib], xbuf, x_send, x_recv, sibling)
    copy.start()
    copy.wait_recv()
    for k in list(order) + [0]:
        to = lax.rem(z + k, ZS)
        rows = pl.ds(pl.multiple_of(to * ROWS, ROWS), ROWS)
        for a in range(2):
            value = acc[c, a, rows] + xbuf[a, rows]
            if k == 0:
                zown[a] = value
            else:
                zsend[k - 1, a] = value.astype(BF16)
        if k:
            remote(zsend.at[k - 1], zrecv.at[k - 1], z_send, z_recv, at_z(k)).start()
    drain(zrecv, z_recv)
    for a, out in enumerate((layer_out, grad_tokens)):
        value = zown[a]
        for k in range(ZS - 1):
            value = value + zrecv[k, a].astype(F32)
        out[...] = value.astype(BF16)

    drain(zrecv, z_send)
    copy.wait_send()
    for copy in z_copies:
        copy.wait_send()
    for copy in to_sib:
        copy.wait_send()

    @pl.loop(0, NR)
    def _(r):
        for h in range(2):
            drain(recv1.at[r, h], send1.at[r, h])
            drain(recv2.at[r, h], send2.at[r, h])
            drain(recv2.at[r, h], send3.at[r, h])
            drain(recv1.at[r, h], send4.at[r, h])
        for copy in outs(r):
            copy.wait()


def local(tokens, grad_out, gate_weight, up_weight, down_weight, gate_mask, up_mask, down_mask):
    any_spec = pl.BlockSpec(memory_space=pl.ANY)
    vmem = pl.BlockSpec(memory_space=pltpu.VMEM)
    smem = pl.BlockSpec(memory_space=pltpu.SMEM)
    dma = pltpu.SemaphoreType.DMA
    block = (3, ROWS, LANES)
    return pl.pallas_call(
        kernel,
        name="sparse_swiglu_step",
        out_shape=[
            jax.ShapeDtypeStruct((ROWS, WID), BF16),
            jax.ShapeDtypeStruct((ROWS, WID), BF16),
            jax.ShapeDtypeStruct((WID, HID), BF16),
            jax.ShapeDtypeStruct((WID, HID), BF16),
            jax.ShapeDtypeStruct((HID, WID), BF16),
        ],
        in_specs=[any_spec] * 5 + [smem] * 3,
        out_specs=[vmem, vmem, any_spec, any_spec, any_spec],
        scratch_shapes=[
            pltpu.VMEM((2 * ZS, 2, ROWS, WID), BF16),
            pltpu.VMEM((WID, TOK), BF16),
            pltpu.VMEM((NR, WID, CH), BF16),
            pltpu.VMEM((NR, WID, CH), BF16),
            pltpu.VMEM((NR, CH, WID), BF16),
            pltpu.VMEM((NR, 2, GROUP) + block, BF16),
            pltpu.VMEM((2, 2, GROUP) + block, F32),
            pltpu.VMEM((NR, 2, SIDE - 1, SIDE) + block, BF16),
            pltpu.VMEM((NR, 2, SIDE) + block, BF16),
            pltpu.VMEM((2, 2, SIDE) + block, F32),
            pltpu.VMEM((NR, 2, SIDE - 1) + block, BF16),
            pltpu.VMEM((NR, 2, GROUP) + block, BF16),
            pltpu.VMEM((NR, WID, CH), BF16),
            pltpu.VMEM((NR, WID, CH), BF16),
            pltpu.VMEM((NR, CH, WID), BF16),
            pltpu.VMEM((2, 2, TOK // 2, WID), F32),
            pltpu.VMEM((2, TOK // 2, WID), F32),
            pltpu.VMEM((ZS - 1, 2, ROWS, WID), BF16),
            pltpu.VMEM((2, ROWS, WID), F32),
            pltpu.VMEM((ZS - 1, 2, ROWS, WID), BF16),
            dma((2,)),
            dma((3, NR)),
            dma((ZS - 1,)), dma((ZS - 1,)),
            dma((ZS,)), dma,
            dma((NR, 2)), dma((NR, 2)),
            dma((NR, 2)), dma((NR, 2)),
            dma((NR, 2)), dma((NR, 2)),
            dma((NR, 2)), dma((NR, 2)),
            dma((3, NR)),
            dma, dma, dma, dma,
        ],
        compiler_params=pltpu.CompilerParams(
            collective_id=0, has_side_effects=True, vmem_limit_bytes=56 << 20
        ),
    )(tokens, grad_out, gate_weight, up_weight, down_weight, gate_mask, up_mask, down_mask)


def solution(mesh):
    wide, tall = P("inb", "outb"), P("outb", "inb")
    return jax.shard_map(
        local,
        mesh=mesh,
        in_specs=(tall, tall, wide, wide, tall, wide, wide, tall),
        out_specs=(tall, tall, wide, wide, tall),
        check_vma=False,
    )
```

```python
import functools

import jax
import jax.numpy as jnp
from jax import lax
from jax.experimental import pallas as pl
from jax.experimental.pallas import tpu as pltpu
from jax.sharding import PartitionSpec as P

MESH = pl.DeviceIdType.MESH
F32 = jnp.float32
BF16 = jnp.bfloat16
SIDE = 4
ZS = 8
GROUP = SIDE * SIDE
ROWS = 32
HALF = ROWS // 2
TOK = GROUP * HALF
WID = 512
HID = 1792
LANES = 128
CH = 2 * LANES
NR = HID // CH
NQ = 2 * NR
LAG = 2
KEEP = LAG + 1
LAST = NQ + 4 * LAG


def dot(a, b):
    return jnp.dot(a, b, preferred_element_type=F32)


def dot_nt(a, b):
    return lax.dot_general(a, b, (((1,), (1,)), ((), ())), preferred_element_type=F32)


def dot_tn(a, b):
    return lax.dot_general(a, b, (((0,), (0,)), ((), ())), preferred_element_type=F32)


def kernel(
    tokens, grad_out, gate_w, up_w, down_w, gate_mask, up_mask, down_mask,
    layer_out, grad_tokens, grad_gate, grad_up, grad_down,
    gate_m, up_m, down_m, ab, tok_t, gw, uw, dw, part, own, recv1, mid, mid_own, recv2, full,
    out_g, out_u, out_d, acc, xbuf, zsend, zown, zrecv,
    load_sem, m_sem, w_sem, a_send, a_recv, s_send, s_recv,
    send1, got1, send2, got2, send3, got3, send4, got4, out_sem,
    x_send, x_recv, z_send, z_recv,
):
    i = lax.axis_index("inb")
    o = lax.axis_index("outb")
    x, y = i // SIDE, lax.rem(i, SIDE)
    z, c = o // 2, lax.rem(o, 2)
    sib = 1 - c

    def at_x(k):
        return (lax.rem(x + k, SIDE) * SIDE + y, o)

    def at_y(k):
        return (x * SIDE + lax.rem(y + k, SIDE), o)

    def at_z(k):
        return (i, lax.rem(z + k, ZS) * 2 + c)

    sibling = (i, z * 2 + sib)

    def remote(src, dst, s, r, device):
        return pltpu.make_async_remote_copy(
            src_ref=src, dst_ref=dst, send_sem=s, recv_sem=r,
            device_id=device, device_id_type=MESH,
        )

    def drain(ref, sem):
        pltpu.make_async_copy(ref, ref, sem).wait()

    mine = c * ZS + z
    first = []
    for th in range(2):
        rows = pl.ds(th * HALF, HALF)
        first.append(pltpu.make_async_copy(tokens.at[rows], ab.at[th, mine, 0], load_sem.at[th, 0]))
        first.append(pltpu.make_async_copy(grad_out.at[rows], ab.at[th, mine, 1], load_sem.at[th, 1]))
    for copy in first:
        copy.start()
    weights = [
        pltpu.make_async_copy(gate_mask, gate_m, m_sem.at[0]),
        pltpu.make_async_copy(up_mask, up_m, m_sem.at[1]),
        pltpu.make_async_copy(down_mask, down_m, m_sem.at[2]),
    ]
    for r in range(NR):
        cols = pl.ds(r * CH, CH)
        weights.append(pltpu.make_async_copy(gate_w.at[:, cols], gw.at[r], w_sem.at[0, r]))
        weights.append(pltpu.make_async_copy(up_w.at[:, cols], uw.at[r], w_sem.at[1, r]))
        weights.append(pltpu.make_async_copy(down_w.at[cols, :], dw.at[r], w_sem.at[2, r]))
    for copy in weights:
        copy.start()

    barrier = pltpu.get_barrier_semaphore()
    for k in range(1, SIDE):
        pl.semaphore_signal(barrier, inc=1, device_id=at_x(k), device_id_type=MESH)
        pl.semaphore_signal(barrier, inc=1, device_id=at_y(k), device_id_type=MESH)
    for k in range(1, ZS):
        pl.semaphore_signal(barrier, inc=1, device_id=at_z(k), device_id_type=MESH)
    pl.semaphore_signal(barrier, inc=1, device_id=sibling, device_id_type=MESH)
    pl.semaphore_wait(barrier, 2 * (SIDE - 1) + ZS - 1 + 1)

    order = (4, 3, 5, 2, 6, 1, 7)
    near = (1, 7, 2, 6, 3, 5, 4)

    def z_copy(th, k):
        block = ab.at[th, mine]
        return remote(block, block, a_send.at[th, k - 1], a_recv.at[th, k - 1], at_z(k))

    def to_sibling(th, k):
        block = ab.at[th, c * ZS + lax.rem(z + ZS - k, ZS)]
        return remote(block, block, s_send.at[th, k], s_recv.at[th], sibling)

    def gather_start(th):
        for k in order:
            z_copy(th, k).start()
        to_sibling(th, 0).start()

    def gather_relay(th):
        for k in near:
            z_copy(th, k).wait_recv()
            to_sibling(th, k).start()

    def gather_end(th):
        drain(ab.at[th, pl.ds(sib * ZS, ZS)], s_recv.at[th])

    for copy in first:
        copy.wait()
    gather_start(0)

    acc[...] = jnp.zeros_like(acc)
    for copy in weights:
        copy.wait()
    for r in range(NR):
        for a in range(WID // LANES):
            for b in range(2):
                rows, cols = pl.ds(a * LANES, LANES), pl.ds(b * LANES, LANES)
                for w, m in ((gw, gate_m), (uw, up_m)):
                    keep = jnp.full((LANES, LANES), m[a, 2 * r + b].astype(F32), F32)
                    w[r, rows, cols] = w[r, rows, cols] * keep.astype(BF16)
                keep = jnp.full((LANES, LANES), down_m[a, 2 * r + b].astype(F32), F32)
                dw[r, cols, rows] = dw[r, cols, rows] * keep.astype(BF16)

    gather_relay(0)
    gather_end(0)
    gather_start(1)

    def places(h):
        return (at_x, at_y, x, y) if h == 0 else (at_y, at_x, y, x)

    def half_of(q):
        th = q // NR
        return th, q - th * NR

    def partial_sums(q):
        th, r = half_of(q)
        tok = ab[th, :, 0].reshape(TOK, WID)
        cot = ab[th, :, 1].reshape(TOK, WID)
        slot = lax.rem(q, KEEP)
        for n in range(3):
            if n == 0:
                value = dot(tok, gw[r])
            elif n == 1:
                value = dot(tok, uw[r])
            else:
                value = dot_nt(cot, dw[r])
            for h in range(2):
                piece = value[:, h * LANES:(h + 1) * LANES].reshape(GROUP, HALF, LANES)
                own[slot, h, :, n] = piece
                part[q, h, :, n] = piece.astype(BF16)
        for h in range(2):
            at1, _, p1, _ = places(h)
            for k in range(1, SIDE):
                to = lax.rem(p1 + k, SIDE)
                remote(
                    part.at[q, h, pl.ds(to * SIDE, SIDE)], recv1.at[q, h, k - 1],
                    send1.at[q, h], got1.at[q, h], at1(k),
                ).start()

    def second(q):
        slot = lax.rem(q, KEEP)
        for h in range(2):
            _, at2, p1, p2 = places(h)
            drain(recv1.at[q, h], got1.at[q, h])
            total = own[slot, h, pl.ds(p1 * SIDE, SIDE)]
            for k in range(SIDE - 1):
                total = total + recv1[q, h, k].astype(F32)
            mid_own[slot, h] = total
            mid[q, h] = total.astype(BF16)
            for k in range(1, SIDE):
                to = lax.rem(p2 + k, SIDE)
                remote(
                    mid.at[q, h, to], recv2.at[q, h, k - 1],
                    send2.at[q, h], got2.at[q, h], at2(k),
                ).start()

    def activations(q):
        slot = lax.rem(q, KEEP)
        for h in range(2):
            _, at2, p1, p2 = places(h)
            drain(recv2.at[q, h], got2.at[q, h])
            total = mid_own[slot, h, p2]
            for k in range(SIDE - 1):
                total = total + recv2[q, h, k].astype(F32)
            gate, up, hidden_grad = total[0], total[1], total[2]
            sig = jax.nn.sigmoid(gate)
            act = gate * sig
            at = p1 * SIDE + p2
            full[q, h, at, 0] = (act * up).astype(BF16)
            full[q, h, at, 1] = (hidden_grad * up * sig * (1.0 + gate * (1.0 - sig))).astype(BF16)
            full[q, h, at, 2] = (hidden_grad * act).astype(BF16)
            for k in range(1, SIDE):
                block = full.at[q, h, at]
                remote(block, block, send3.at[q, h], got3.at[q, h], at2(k)).start()

    def spread(q):
        for h in range(2):
            at1, _, p1, _ = places(h)
            drain(recv2.at[q, h], got3.at[q, h])
            for k in range(1, SIDE):
                block = full.at[q, h, pl.ds(p1 * SIDE, SIDE)]
                remote(block, block, send4.at[q, h], got4.at[q, h], at1(k)).start()

    def whole(q, n):
        return jnp.concatenate(
            [full[q, h, :, n].reshape(TOK, LANES) for h in range(2)], axis=1
        )

    def finish(q):
        th, r = half_of(q)
        drain(recv1.at[q, 0], got4.at[q, 0])
        drain(recv1.at[q, 1], got4.at[q, 1])
        hidden, gate_grad, up_grad = whole(q, 0), whole(q, 1), whole(q, 2)
        half = TOK // 2
        value = dot(hidden, dw[r])
        acc[th, 0, 0] += value[:half]
        acc[th, 1, 0] += value[half:]
        value = dot_nt(gate_grad, gw[r]) + dot_nt(up_grad, uw[r])
        acc[th, 0, 1] += value[:half]
        acc[th, 1, 1] += value[half:]

        @pl.when(r == NR - 1)
        def _():
            cores_start(th)

    def weight_grads(r):
        for out, n, m in ((out_g, 1, gate_m), (out_u, 2, up_m)):
            value = dot(tok_t[0], whole(r, n)) + dot(tok_t[1], whole(r + NR, n))
            for a in range(WID // LANES):
                for b in range(2):
                    rows, cols = slice(a * LANES, (a + 1) * LANES), slice(b * LANES, (b + 1) * LANES)
                    keep = m[a, 2 * r + b].astype(F32)
                    out[r, rows, cols] = (value[rows, cols] * keep).astype(BF16)
        value = dot_tn(whole(r, 0), ab[0, :, 1].reshape(TOK, WID))
        value = value + dot_tn(whole(r + NR, 0), ab[1, :, 1].reshape(TOK, WID))
        for a in range(WID // LANES):
            for b in range(2):
                rows, cols = slice(a * LANES, (a + 1) * LANES), slice(b * LANES, (b + 1) * LANES)
                keep = down_m[a, 2 * r + b].astype(F32)
                out_d[r, cols, rows] = (value[cols, rows] * keep).astype(BF16)
        for copy in outs(r):
            copy.start()

    def outs(r):
        cols = pl.ds(pl.multiple_of(r * CH, CH), CH)
        return [
            pltpu.make_async_copy(out_g.at[r], grad_gate.at[:, cols], out_sem.at[0, r]),
            pltpu.make_async_copy(out_u.at[r], grad_up.at[:, cols], out_sem.at[1, r]),
            pltpu.make_async_copy(out_d.at[r], grad_down.at[cols, :], out_sem.at[2, r]),
        ]

    def cores_copy(th):
        return remote(acc.at[th, sib], xbuf.at[th], x_send.at[th], x_recv.at[th], sibling)

    def cores_start(th):
        cores_copy(th).start()

    def z_start(th):
        cores_copy(th).wait_recv()
        for k in order + (0,):
            to = lax.rem(z + k, ZS)
            rows = pl.ds(pl.multiple_of(to * HALF, HALF), HALF)
            for a in range(2):
                value = acc[th, c, a, rows] + xbuf[th, a, rows]
                if k == 0:
                    zown[th, a] = value
                else:
                    zsend[th, k - 1, a] = value.astype(BF16)
            if k:
                remote(
                    zsend.at[th, k - 1], zrecv.at[th, k - 1], z_send.at[th], z_recv.at[th], at_z(k)
                ).start()

    def z_end(th):
        drain(zrecv.at[th], z_recv.at[th])
        for a, out in enumerate((layer_out, grad_tokens)):
            value = zown[th, a]
            for k in range(ZS - 1):
                value = value + zrecv[th, k, a].astype(F32)
            out[pl.ds(th * HALF, HALF)] = value.astype(BF16)

    @pl.loop(0, LAST)
    def _(t):
        def stage(s, work):
            @pl.when(jnp.logical_and(t >= s * LAG, t < NQ + s * LAG))
            def _():
                work(t - s * LAG)

        stage(1, second)
        stage(2, activations)
        stage(3, spread)

        @pl.when(t == NR - 1)
        def _():
            gather_relay(1)

        @pl.when(t == NR)
        def _():
            gather_end(1)

        stage(0, partial_sums)

        @pl.when(t == NR + 1)
        def _():
            for th in range(2):
                tok_t[th] = ab[th, :, 0].reshape(TOK, WID).T

        stage(4, finish)

        @pl.when(t >= NR + 4 * LAG)
        def _():
            weight_grads(t - NR - 4 * LAG)

        @pl.when(t == NR + 4 * LAG)
        def _():
            z_start(0)

    z_start(1)
    z_end(0)
    z_end(1)

    for th in range(2):
        drain(zrecv.at[th], z_send.at[th])
        cores_copy(th).wait_send()
        for k in range(ZS):
            if k:
                z_copy(th, k).wait_send()
            to_sibling(th, k).wait_send()

    @pl.loop(0, NQ)
    def _(q):
        for h in range(2):
            drain(recv1.at[q, h], send1.at[q, h])
            drain(recv2.at[q, h], send2.at[q, h])
            drain(recv2.at[q, h], send3.at[q, h])
            drain(recv1.at[q, h], send4.at[q, h])

    @pl.loop(0, NR)
    def _(r):
        for copy in outs(r):
            copy.wait()


def hand_over(*refs):
    n = len(refs) // 2
    sem = refs[-1]
    copies = [pltpu.make_async_copy(refs[j], refs[n + j], sem.at[j]) for j in range(n)]
    for copy in copies:
        copy.start()
    for copy in copies:
        copy.wait()


def local(tokens, grad_out, gate_weight, up_weight, down_weight, gate_mask, up_mask, down_mask):
    any_spec = pl.BlockSpec(memory_space=pl.ANY)
    vmem = pl.BlockSpec(memory_space=pltpu.VMEM)
    hbm = pl.BlockSpec(memory_space=pltpu.HBM)
    dma = pltpu.SemaphoreType.DMA
    block = (3, HALF, LANES)
    shapes = [
        jax.ShapeDtypeStruct((ROWS, WID), BF16),
        jax.ShapeDtypeStruct((ROWS, WID), BF16),
        jax.ShapeDtypeStruct((WID, HID), BF16),
        jax.ShapeDtypeStruct((WID, HID), BF16),
        jax.ShapeDtypeStruct((HID, WID), BF16),
    ]
    results = pl.pallas_call(
        kernel,
        name="sparse_swiglu_step",
        out_shape=shapes,
        in_specs=[hbm] * 8,
        out_specs=[vmem, vmem, any_spec, any_spec, any_spec],
        scratch_shapes=[
            pltpu.SMEM((WID // LANES, HID // LANES), jnp.int32),
            pltpu.SMEM((WID // LANES, HID // LANES), jnp.int32),
            pltpu.SMEM((WID // LANES, HID // LANES), jnp.int32),
            pltpu.VMEM((2, 2 * ZS, 2, HALF, WID), BF16),
            pltpu.VMEM((2, WID, TOK), BF16),
            pltpu.VMEM((NR, WID, CH), BF16),
            pltpu.VMEM((NR, WID, CH), BF16),
            pltpu.VMEM((NR, CH, WID), BF16),
            pltpu.VMEM((NQ, 2, GROUP) + block, BF16),
            pltpu.VMEM((KEEP, 2, GROUP) + block, F32),
            pltpu.VMEM((NQ, 2, SIDE - 1, SIDE) + block, BF16),
            pltpu.VMEM((NQ, 2, SIDE) + block, BF16),
            pltpu.VMEM((KEEP, 2, SIDE) + block, F32),
            pltpu.VMEM((NQ, 2, SIDE - 1) + block, BF16),
            pltpu.VMEM((NQ, 2, GROUP) + block, BF16),
            pltpu.VMEM((NR, WID, CH), BF16),
            pltpu.VMEM((NR, WID, CH), BF16),
            pltpu.VMEM((NR, CH, WID), BF16),
            pltpu.VMEM((2, 2, 2, TOK // 2, WID), F32),
            pltpu.VMEM((2, 2, TOK // 2, WID), F32),
            pltpu.VMEM((2, ZS - 1, 2, HALF, WID), BF16),
            pltpu.VMEM((2, 2, HALF, WID), F32),
            pltpu.VMEM((2, ZS - 1, 2, HALF, WID), BF16),
            dma((2, 2)),
            dma((3,)),
            dma((3, NR)),
            dma((2, ZS - 1)), dma((2, ZS - 1)),
            dma((2, ZS)), dma((2,)),
            dma((NQ, 2)), dma((NQ, 2)),
            dma((NQ, 2)), dma((NQ, 2)),
            dma((NQ, 2)), dma((NQ, 2)),
            dma((NQ, 2)), dma((NQ, 2)),
            dma((3, NR)),
            dma((2,)), dma((2,)), dma((2,)), dma((2,)),
        ],
        compiler_params=pltpu.CompilerParams(
            collective_id=0, has_side_effects=True, vmem_limit_bytes=48 << 20
        ),
    )(*(
        pltpu.with_memory_space_constraint(value, pltpu.HBM)
        for value in (
            tokens, grad_out, gate_weight, up_weight, down_weight, gate_mask, up_mask, down_mask.T
        )
    ))
    return pl.pallas_call(
        hand_over,
        name="hand_over",
        out_shape=shapes,
        in_specs=[any_spec] * 5,
        out_specs=[any_spec] * 5,
        scratch_shapes=[dma((5,))],
        compiler_params=pltpu.CompilerParams(vmem_limit_bytes=1 << 20),
    )(*results)


def solution(mesh):
    wide, tall = P("inb", "outb"), P("outb", "inb")
    return jax.shard_map(
        local,
        mesh=mesh,
        in_specs=(tall, tall, wide, wide, tall, wide, wide, tall),
        out_specs=(tall, tall, wide, wide, tall),
        check_vma=False,
    )
```

```python
import functools

import jax
import jax.numpy as jnp
from jax import lax
from jax.experimental import pallas as pl
from jax.experimental.pallas import tpu as pltpu
from jax.sharding import PartitionSpec as P

MESH = pl.DeviceIdType.MESH
F32 = jnp.float32
BF16 = jnp.bfloat16
SIDE = 4
ZS = 8
GROUP = SIDE * SIDE
ROWS = 32
HALF = ROWS // 2
PAIR = SIDE // 2
TOK = GROUP * HALF
WID = 512
HID = 1792
LANES = 128
CH = 2 * LANES
NR = HID // CH
NQ = 2 * NR
LAG = 2
KEEP = LAG + 1
KEEP_OWN = 2 * LAG + 1
STAGES = 7
LAST = NQ + (STAGES - 1) * LAG


def dot(a, b):
    return jnp.dot(a, b, preferred_element_type=F32)


def dot_nt(a, b):
    return lax.dot_general(a, b, (((1,), (1,)), ((), ())), preferred_element_type=F32)


def dot_tn(a, b):
    return lax.dot_general(a, b, (((0,), (0,)), ((), ())), preferred_element_type=F32)


def kernel(
    tokens, grad_out, gate_w, up_w, down_w, gate_mask, up_mask, down_mask,
    layer_out, grad_tokens, grad_gate, grad_up, grad_down,
    gate_m, up_m, down_m, ab, tok_t, gw, uw, dw, part, own, recv1, mid, mid_own, recv2, full,
    chain, out_g, out_u, out_d, acc, xbuf, zown, zsend_0, zsend_1, zrecv_0, zrecv_1,
    load_sem, m_sem, w_sem, a_send, a_recv, s_send, s_recv,
    send1, got0, got1, send2, got2, send3, got3, send4, got4, got5, out_sem,
    x_send, x_recv, z_send, z_recv,
):
    i = lax.axis_index("inb")
    o = lax.axis_index("outb")
    x, y = i // SIDE, lax.rem(i, SIDE)
    z, c = o // 2, lax.rem(o, 2)
    sib = 1 - c

    def at_x(k):
        return (lax.rem(x + k, SIDE) * SIDE + y, o)

    def at_y(k):
        return (x * SIDE + lax.rem(y + k, SIDE), o)

    def at_z(k):
        return (i, lax.rem(z + k, ZS) * 2 + c)

    sibling = (i, z * 2 + sib)

    def remote(src, dst, s, r, device):
        return pltpu.make_async_remote_copy(
            src_ref=src, dst_ref=dst, send_sem=s, recv_sem=r,
            device_id=device, device_id_type=MESH,
        )

    def drain(ref, sem):
        pltpu.make_async_copy(ref, ref, sem).wait()

    mine = c * ZS + z
    first = []
    for th in range(2):
        rows = pl.ds(th * HALF, HALF)
        first.append(pltpu.make_async_copy(tokens.at[rows], ab.at[th, mine, 0], load_sem.at[th, 0]))
        first.append(pltpu.make_async_copy(grad_out.at[rows], ab.at[th, mine, 1], load_sem.at[th, 1]))
    for copy in first:
        copy.start()
    weights = [
        pltpu.make_async_copy(gate_mask, gate_m, m_sem.at[0]),
        pltpu.make_async_copy(up_mask, up_m, m_sem.at[1]),
        pltpu.make_async_copy(down_mask, down_m, m_sem.at[2]),
    ]
    for r in range(NR):
        cols = pl.ds(r * CH, CH)
        weights.append(pltpu.make_async_copy(gate_w.at[:, cols], gw.at[r], w_sem.at[0, r]))
        weights.append(pltpu.make_async_copy(up_w.at[:, cols], uw.at[r], w_sem.at[1, r]))
        weights.append(pltpu.make_async_copy(down_w.at[cols, :], dw.at[r], w_sem.at[2, r]))
    for copy in weights:
        copy.start()

    barrier = pltpu.get_barrier_semaphore()
    for k in range(1, SIDE):
        pl.semaphore_signal(barrier, inc=1, device_id=at_x(k), device_id_type=MESH)
        pl.semaphore_signal(barrier, inc=1, device_id=at_y(k), device_id_type=MESH)
    for k in range(1, ZS):
        pl.semaphore_signal(barrier, inc=1, device_id=at_z(k), device_id_type=MESH)
    pl.semaphore_signal(barrier, inc=1, device_id=sibling, device_id_type=MESH)
    pl.semaphore_wait(barrier, 2 * (SIDE - 1) + ZS - 1 + 1)

    order = (4, 3, 5, 2, 6, 1, 7)
    near = (1, 7, 2, 6, 3, 5, 4)

    def z_copy(th, k):
        block = ab.at[th, mine]
        return remote(block, block, a_send.at[th, k - 1], a_recv.at[th, k - 1], at_z(k))

    def to_sibling(th, k):
        block = ab.at[th, c * ZS + lax.rem(z + ZS - k, ZS)]
        return remote(block, block, s_send.at[th, k], s_recv.at[th], sibling)

    def gather_start(th):
        for k in order:
            z_copy(th, k).start()
        to_sibling(th, 0).start()

    def gather_relay(th):
        for k in near:
            z_copy(th, k).wait_recv()
            to_sibling(th, k).start()

    def gather_end(th):
        drain(ab.at[th, pl.ds(sib * ZS, ZS)], s_recv.at[th])

    for copy in first:
        copy.wait()
    gather_start(0)

    acc[...] = jnp.zeros_like(acc)
    for copy in weights:
        copy.wait()
    for r in range(NR):
        for a in range(WID // LANES):
            for b in range(2):
                rows, cols = pl.ds(a * LANES, LANES), pl.ds(b * LANES, LANES)
                for w, m in ((gw, gate_m), (uw, up_m)):
                    keep = jnp.full((LANES, LANES), m[a, 2 * r + b].astype(F32), F32)
                    w[r, rows, cols] = w[r, rows, cols] * keep.astype(BF16)
                keep = jnp.full((LANES, LANES), down_m[a, 2 * r + b].astype(F32), F32)
                dw[r, cols, rows] = dw[r, cols, rows] * keep.astype(BF16)

    gather_relay(0)
    gather_end(0)
    gather_start(1)

    def places(h):
        return (at_x, at_y, x, y) if h == 0 else (at_y, at_x, y, x)

    def half_of(q):
        th = q // NR
        return th, q - th * NR

    def partial_sums(q):
        th, r = half_of(q)
        tok = ab[th, :, 0].reshape(TOK, WID)
        cot = ab[th, :, 1].reshape(TOK, WID)
        slot = lax.rem(q, KEEP_OWN)
        for n in range(3):
            if n == 0:
                value = dot(tok, gw[r])
            elif n == 1:
                value = dot(tok, uw[r])
            else:
                value = dot_nt(cot, dw[r])
            for h in range(2):
                piece = value[:, h * LANES:(h + 1) * LANES].reshape(GROUP, HALF, LANES)
                own[slot, h, :, n] = piece
                part[q, h, :, n] = piece.astype(BF16)
        for h in range(2):
            at1, _, p1, _ = places(h)
            after, far, before = (lax.rem(p1 + k, SIDE) * SIDE for k in range(1, SIDE))
            for start, slot_to, sem, k in (
                (far, 0, got0, 1), (far + PAIR, 1, got0, 3),
                (after + PAIR, 2, got1, 1), (before, 3, got1, 3),
            ):
                remote(
                    part.at[q, h, pl.ds(start, PAIR)], recv1.at[q, h, slot_to],
                    send1.at[q, h], sem.at[q, h], at1(k),
                ).start()

    def add_share(q):
        slot = lax.rem(q, KEEP_OWN)
        for h in range(2):
            at1, _, p1, _ = places(h)
            drain(recv1.at[q, h, pl.ds(0, 2)], got0.at[q, h])
            after, before = (lax.rem(p1 + k, SIDE) * SIDE for k in (1, 3))
            for j, start, k in ((0, after, 1), (1, before + PAIR, 3)):
                total = own[slot, h, pl.ds(start, PAIR)] + recv1[q, h, j].astype(F32)
                chain[q, h, j] = total.astype(BF16)
                remote(
                    chain.at[q, h, j], recv1.at[q, h, 4 + j],
                    send1.at[q, h], got1.at[q, h], at1(k),
                ).start()

    def second(q):
        slot = lax.rem(q, KEEP)
        slot_own = lax.rem(q, KEEP_OWN)

        for h in range(2):
            p1 = places(h)[2]
            drain(recv1.at[q, h, pl.ds(2, 4)], got1.at[q, h])
            for half, j in ((0, (3, 4)), (1, (2, 5))):
                total = own[slot_own, h, pl.ds(p1 * SIDE + half * PAIR, PAIR)]
                for n in j:
                    total = total + recv1[q, h, n].astype(F32)
                mid_own[slot, h, pl.ds(half * PAIR, PAIR)] = total
                mid[q, h, pl.ds(half * PAIR, PAIR)] = total.astype(BF16)

        for h in range(2):
            _, at2, _, p2 = places(h)
            for k in range(1, SIDE):
                to = lax.rem(p2 + k, SIDE)
                remote(
                    mid.at[q, h, to], recv2.at[q, h, k - 1],
                    send2.at[q, h], got2.at[q, h], at2(k),
                ).start()

    def activations(q):
        slot = lax.rem(q, KEEP)
        for h in range(2):
            _, at2, p1, p2 = places(h)
            drain(recv2.at[q, h], got2.at[q, h])
            total = mid_own[slot, h, p2]
            for k in range(SIDE - 1):
                total = total + recv2[q, h, k].astype(F32)
            gate, up, hidden_grad = total[0], total[1], total[2]
            sig = jax.nn.sigmoid(gate)
            act = gate * sig
            at = p1 * SIDE + p2
            full[q, h, at, 0] = (act * up).astype(BF16)
            full[q, h, at, 1] = (hidden_grad * up * sig * (1.0 + gate * (1.0 - sig))).astype(BF16)
            full[q, h, at, 2] = (hidden_grad * act).astype(BF16)
            for k in range(1, SIDE):
                block = full.at[q, h, at]
                remote(block, block, send3.at[q, h], got3.at[q, h], at2(k)).start()

    def spread(q):
        for h in range(2):
            at1, _, p1, _ = places(h)
            drain(recv2.at[q, h], got3.at[q, h])
            block = full.at[q, h, pl.ds(p1 * SIDE, SIDE)]
            for k in (1, 3):
                remote(block, block, send4.at[q, h], got4.at[q, h], at1(k)).start()

    def forward(q):
        for h in range(2):
            at1, _, p1, _ = places(h)
            drain(recv1.at[q, h, pl.ds(0, 4)], got4.at[q, h])

            after, before = (lax.rem(p1 + k, SIDE) * SIDE for k in (1, 3))
            for start, k in ((before, 1), (after + PAIR, 3)):
                block = full.at[q, h, pl.ds(start, PAIR)]
                remote(block, block, send4.at[q, h], got5.at[q, h], at1(k)).start()

    def whole(q, n):
        return jnp.concatenate(
            [full[q, h, :, n].reshape(TOK, LANES) for h in range(2)], axis=1
        )

    def finish(q):
        th, r = half_of(q)
        for h in range(2):
            drain(recv1.at[q, h, pl.ds(0, 2)], got5.at[q, h])
        hidden, gate_grad, up_grad = whole(q, 0), whole(q, 1), whole(q, 2)
        half = TOK // 2
        value = dot(hidden, dw[r])
        acc[th, 0, 0] += value[:half]
        acc[th, 1, 0] += value[half:]
        value = dot_nt(gate_grad, gw[r]) + dot_nt(up_grad, uw[r])
        acc[th, 0, 1] += value[:half]
        acc[th, 1, 1] += value[half:]

        @pl.when(r == NR - 1)
        def _():
            cores_start(th)

    def weight_grads(r):
        for out, n, m in ((out_g, 1, gate_m), (out_u, 2, up_m)):
            value = dot(tok_t[0], whole(r, n)) + dot(tok_t[1], whole(r + NR, n))
            for a in range(WID // LANES):
                for b in range(2):
                    rows, cols = slice(a * LANES, (a + 1) * LANES), slice(b * LANES, (b + 1) * LANES)
                    keep = m[a, 2 * r + b].astype(F32)
                    out[r, rows, cols] = (value[rows, cols] * keep).astype(BF16)
        value = dot_tn(whole(r, 0), ab[0, :, 1].reshape(TOK, WID))
        value = value + dot_tn(whole(r + NR, 0), ab[1, :, 1].reshape(TOK, WID))
        for a in range(WID // LANES):
            for b in range(2):
                rows, cols = slice(a * LANES, (a + 1) * LANES), slice(b * LANES, (b + 1) * LANES)
                keep = down_m[a, 2 * r + b].astype(F32)
                out_d[r, cols, rows] = (value[cols, rows] * keep).astype(BF16)
        for copy in outs(r):
            copy.start()

    def outs(r):
        cols = pl.ds(pl.multiple_of(r * CH, CH), CH)
        return [
            pltpu.make_async_copy(out_g.at[r], grad_gate.at[:, cols], out_sem.at[0, r]),
            pltpu.make_async_copy(out_u.at[r], grad_up.at[:, cols], out_sem.at[1, r]),
            pltpu.make_async_copy(out_d.at[r], grad_down.at[cols, :], out_sem.at[2, r]),
        ]

    def cores_copy(th):
        return remote(acc.at[th, sib], xbuf.at[th], x_send.at[th], x_recv.at[th], sibling)

    def cores_start(th):
        cores_copy(th).start()

    zsend, zrecv = (zsend_0, zsend_1), (zrecv_0, zrecv_1)

    def z_start(th):
        cores_copy(th).wait_recv()
        for k in order + (0,):
            to = lax.rem(z + k, ZS)
            rows = pl.ds(pl.multiple_of(to * HALF, HALF), HALF)
            for a in range(2):
                value = acc[th, c, a, rows] + xbuf[th, a, rows]
                if k == 0:
                    zown[th, a] = value
                else:
                    zsend[th][k - 1, a] = value.astype(zsend[th].dtype)
            if k:
                remote(
                    zsend[th].at[k - 1], zrecv[th].at[k - 1], z_send.at[th], z_recv.at[th], at_z(k)
                ).start()

    def z_end(th):
        drain(zrecv[th], z_recv.at[th])
        for a, out in enumerate((layer_out, grad_tokens)):
            value = zown[th, a]
            for k in range(ZS - 1):
                value = value + zrecv[th][k, a].astype(F32)
            out[pl.ds(th * HALF, HALF)] = value.astype(BF16)

    @pl.loop(0, LAST)
    def _(t):
        def stage(s, work):
            @pl.when(jnp.logical_and(t >= s * LAG, t < NQ + s * LAG))
            def _():
                work(t - s * LAG)

        stage(1, add_share)
        stage(2, second)
        stage(3, activations)
        stage(4, spread)
        stage(5, forward)

        @pl.when(t == NR - 1)
        def _():
            gather_relay(1)

        @pl.when(t == NR)
        def _():
            gather_end(1)

        stage(0, partial_sums)

        @pl.when(t == NR + 1)
        def _():
            for th in range(2):
                tok_t[th] = ab[th, :, 0].reshape(TOK, WID).T

        stage(6, finish)

        @pl.when(t >= NR + 6 * LAG)
        def _():
            weight_grads(t - NR - 6 * LAG)

        @pl.when(t == NR + 6 * LAG)
        def _():
            z_start(0)

    z_start(1)
    z_end(0)
    z_end(1)

    for th in range(2):
        drain(zrecv[th], z_send.at[th])
        cores_copy(th).wait_send()
        for k in range(ZS):
            if k:
                z_copy(th, k).wait_send()
            to_sibling(th, k).wait_send()

    @pl.loop(0, NQ)
    def _(q):
        for h in range(2):
            drain(recv1.at[q, h], send1.at[q, h])
            drain(recv2.at[q, h], send2.at[q, h])
            drain(recv2.at[q, h], send3.at[q, h])
            drain(recv1.at[q, h], send4.at[q, h])

    @pl.loop(0, NR)
    def _(r):
        for copy in outs(r):
            copy.wait()


def hand_over(*refs):
    n = len(refs) // 2
    sem = refs[-1]
    copies = [pltpu.make_async_copy(refs[j], refs[n + j], sem.at[j]) for j in range(n)]
    for copy in copies:
        copy.start()
    for copy in copies:
        copy.wait()


def local(tokens, grad_out, gate_weight, up_weight, down_weight, gate_mask, up_mask, down_mask):
    any_spec = pl.BlockSpec(memory_space=pl.ANY)
    vmem = pl.BlockSpec(memory_space=pltpu.VMEM)
    hbm = pl.BlockSpec(memory_space=pltpu.HBM)
    dma = pltpu.SemaphoreType.DMA
    block = (3, HALF, LANES)
    shapes = [
        jax.ShapeDtypeStruct((ROWS, WID), BF16),
        jax.ShapeDtypeStruct((ROWS, WID), BF16),
        jax.ShapeDtypeStruct((WID, HID), BF16),
        jax.ShapeDtypeStruct((WID, HID), BF16),
        jax.ShapeDtypeStruct((HID, WID), BF16),
    ]
    results = pl.pallas_call(
        kernel,
        name="sparse_swiglu_step",
        out_shape=shapes,
        in_specs=[hbm] * 8,
        out_specs=[vmem, vmem, any_spec, any_spec, any_spec],
        scratch_shapes=[
            pltpu.SMEM((WID // LANES, HID // LANES), jnp.int32),
            pltpu.SMEM((WID // LANES, HID // LANES), jnp.int32),
            pltpu.SMEM((WID // LANES, HID // LANES), jnp.int32),
            pltpu.VMEM((2, 2 * ZS, 2, HALF, WID), BF16),
            pltpu.VMEM((2, WID, TOK), BF16),
            pltpu.VMEM((NR, WID, CH), BF16),
            pltpu.VMEM((NR, WID, CH), BF16),
            pltpu.VMEM((NR, CH, WID), BF16),
            pltpu.VMEM((NQ, 2, GROUP) + block, BF16),
            pltpu.VMEM((KEEP_OWN, 2, GROUP) + block, F32),
            pltpu.VMEM((NQ, 2, 6, PAIR) + block, BF16),
            pltpu.VMEM((NQ, 2, SIDE) + block, BF16),
            pltpu.VMEM((KEEP, 2, SIDE) + block, F32),
            pltpu.VMEM((NQ, 2, SIDE - 1) + block, BF16),
            pltpu.VMEM((NQ, 2, GROUP) + block, BF16),
            pltpu.VMEM((NQ, 2, 2, PAIR) + block, BF16),
            pltpu.VMEM((NR, WID, CH), BF16),
            pltpu.VMEM((NR, WID, CH), BF16),
            pltpu.VMEM((NR, CH, WID), BF16),
            pltpu.VMEM((2, 2, 2, TOK // 2, WID), F32),
            pltpu.VMEM((2, 2, TOK // 2, WID), F32),
            pltpu.VMEM((2, 2, HALF, WID), F32),
            pltpu.VMEM((ZS - 1, 2, HALF, WID), F32),
            pltpu.VMEM((ZS - 1, 2, HALF, WID), BF16),
            pltpu.VMEM((ZS - 1, 2, HALF, WID), F32),
            pltpu.VMEM((ZS - 1, 2, HALF, WID), BF16),
            dma((2, 2)),
            dma((3,)),
            dma((3, NR)),
            dma((2, ZS - 1)), dma((2, ZS - 1)),
            dma((2, ZS)), dma((2,)),
            dma((NQ, 2)), dma((NQ, 2)), dma((NQ, 2)),
            dma((NQ, 2)), dma((NQ, 2)),
            dma((NQ, 2)), dma((NQ, 2)),
            dma((NQ, 2)), dma((NQ, 2)), dma((NQ, 2)),
            dma((3, NR)),
            dma((2,)), dma((2,)), dma((2,)), dma((2,)),
        ],
        compiler_params=pltpu.CompilerParams(
            collective_id=0, has_side_effects=True, vmem_limit_bytes=48 << 20
        ),
    )(*(
        pltpu.with_memory_space_constraint(value, pltpu.HBM)
        for value in (
            tokens, grad_out, gate_weight, up_weight, down_weight, gate_mask, up_mask, down_mask.T
        )
    ))
    return pl.pallas_call(
        hand_over,
        name="hand_over",
        out_shape=shapes,
        in_specs=[any_spec] * 5,
        out_specs=[any_spec] * 5,
        scratch_shapes=[dma((5,))],
        compiler_params=pltpu.CompilerParams(vmem_limit_bytes=1 << 20),
    )(*results)


def solution(mesh):
    wide, tall = P("inb", "outb"), P("outb", "inb")
    return jax.shard_map(
        local,
        mesh=mesh,
        in_specs=(tall, tall, wide, wide, tall, wide, wide, tall),
        out_specs=(tall, tall, wide, wide, tall),
        check_vma=False,
    )
```

```python
import functools

import jax
import jax.numpy as jnp
from jax import lax
from jax.experimental import pallas as pl
from jax.experimental.pallas import tpu as pltpu
from jax.sharding import PartitionSpec as P

MESH = pl.DeviceIdType.MESH
F32 = jnp.float32
BF16 = jnp.bfloat16
SIDE = 4
ZS = 8
GROUP = SIDE * SIDE
ROWS = 32
HALF = ROWS // 2
PAIR = SIDE // 2
TOK = GROUP * HALF
WID = 512
HID = 1792
LANES = 128
CH = 2 * LANES
NR = HID // CH
NQ = 2 * NR
LAG = 3
KEEP = LAG + 1
KEEP_OWN = 2 * LAG + 1
STAGES = 7
EARLY = 1
WAIT = NR - EARLY
LAST = NQ + WAIT + (STAGES - 1) * LAG
NEAR = ((0, 0, 2, 0), (1, 2, 2, 0), (7, 4, 2, 0), (2, 6, 1, 0), (6, 7, 1, 0))
FAR = ((3, 0, 2, 0), (5, 2, 2, 0), (4, 4, 2, 0), (2, 6, 1, 1), (6, 7, 1, 1))
PIECES = (NEAR, FAR)
WIDE = ((1, 2), (3, 4))
ROWS_WIDE = ((2 * HALF, 4 * HALF), (6 * HALF, 2 * HALF))
ROWS_NARROW = ((6 * HALF, 2 * HALF), (0, 6 * HALF))


def dot(a, b):
    return jnp.dot(a, b, preferred_element_type=F32)


def dot_nt(a, b):
    return lax.dot_general(a, b, (((1,), (1,)), ((), ())), preferred_element_type=F32)


def dot_tn(a, b):
    return lax.dot_general(a, b, (((0,), (0,)), ((), ())), preferred_element_type=F32)


def kernel(
    tokens, grad_out, gate_w, up_w, down_w, gate_mask, up_mask, down_mask,
    layer_out, grad_tokens, grad_gate, grad_up, grad_down,
    gate_m, up_m, down_m, ab, tok_t, gw, uw, dw, part, own, recv1, mid, mid_own, recv2, full,
    chain, out_g, out_u, out_d, acc, xbuf, zown, zsend_n, zsend_w, zrecv_n, zrecv_w,
    load_sem, m_sem, w_sem, a_send, a_recv, s_send, s_recv,
    send1, got0, got1, send2, got2, send3, got3, send4, got4, got5, out_sem,
    x_send, x_recv, z_send, z_recv,
):
    i = lax.axis_index("inb")
    o = lax.axis_index("outb")
    x, y = i // SIDE, lax.rem(i, SIDE)
    z, c = o // 2, lax.rem(o, 2)
    sib = 1 - c

    def at_x(k):
        return (lax.rem(x + k, SIDE) * SIDE + y, o)

    def at_y(k):
        return (x * SIDE + lax.rem(y + k, SIDE), o)

    def at_z(k):
        return (i, lax.rem(z + k, ZS) * 2 + c)

    sibling = (i, z * 2 + sib)

    def remote(src, dst, s, r, device):
        return pltpu.make_async_remote_copy(
            src_ref=src, dst_ref=dst, send_sem=s, recv_sem=r,
            device_id=device, device_id_type=MESH,
        )

    def drain(ref, sem):
        pltpu.make_async_copy(ref, ref, sem).wait()

    first = []
    for half in range(2):
        rows = pl.ds(half * HALF, HALF)
        first.append(pltpu.make_async_copy(tokens.at[rows], ab.at[0, c * ZS + half, 0], load_sem.at[half, 0]))
        first.append(pltpu.make_async_copy(grad_out.at[rows], ab.at[0, c * ZS + half, 1], load_sem.at[half, 1]))
    for copy in first:
        copy.start()
    masks = [
        pltpu.make_async_copy(gate_mask, gate_m, m_sem.at[0]),
        pltpu.make_async_copy(up_mask, up_m, m_sem.at[1]),
        pltpu.make_async_copy(down_mask, down_m, m_sem.at[2]),
    ]
    for copy in masks:
        copy.start()

    def weights(r):
        cols = pl.ds(pl.multiple_of(r * CH, CH), CH)
        return [
            pltpu.make_async_copy(gate_w.at[:, cols], gw.at[r], w_sem.at[0, r]),
            pltpu.make_async_copy(up_w.at[:, cols], uw.at[r], w_sem.at[1, r]),
            pltpu.make_async_copy(down_w.at[cols, :], dw.at[r], w_sem.at[2, r]),
        ]

    @pl.loop(0, NR)
    def _(r):
        for copy in weights(r):
            copy.start()

    barrier = pltpu.get_barrier_semaphore()
    for k in range(1, SIDE):
        pl.semaphore_signal(barrier, inc=1, device_id=at_x(k), device_id_type=MESH)
        pl.semaphore_signal(barrier, inc=1, device_id=at_y(k), device_id_type=MESH)
    for k in range(1, ZS):
        pl.semaphore_signal(barrier, inc=1, device_id=at_z(k), device_id_type=MESH)
    pl.semaphore_signal(barrier, inc=1, device_id=sibling, device_id_type=MESH)
    pl.semaphore_wait(barrier, 2 * (SIDE - 1) + ZS - 1 + 1)

    def z_copy(th, p):
        k, block, n, half = PIECES[th][p]
        return remote(
            ab.at[0, pl.ds(c * ZS + half, n)], ab.at[th, pl.ds(c * ZS + block, n)],
            a_send.at[th, p], a_recv.at[th, p], at_z(ZS - k),
        )

    def to_sibling(th, p):
        _, block, n, _ = PIECES[th][p]
        part_of = ab.at[th, pl.ds(c * ZS + block, n)]
        return remote(part_of, part_of, s_send.at[th, p], s_recv.at[th], sibling)

    def gather_start(th):
        for p, piece in enumerate(PIECES[th]):
            if piece[0]:
                z_copy(th, p).start()
        for p, piece in enumerate(PIECES[th]):
            if not piece[0]:
                to_sibling(th, p).start()

    def gather_relay(th):
        for p, piece in enumerate(PIECES[th]):
            if piece[0]:
                z_copy(th, p).wait_recv()
                to_sibling(th, p).start()

    def gather_end(th):
        drain(ab.at[th, pl.ds(sib * ZS, ZS)], s_recv.at[th])

    for copy in first:
        copy.wait()
    gather_start(0)

    acc[...] = jnp.zeros_like(acc)
    for copy in masks:
        copy.wait()

    def mask_weights(r):
        for copy in weights(r):
            copy.wait()
        for a in range(WID // LANES):
            for b in range(2):
                rows, cols = pl.ds(a * LANES, LANES), pl.ds(b * LANES, LANES)
                for w, m in ((gw, gate_m), (uw, up_m)):
                    keep = jnp.full((LANES, LANES), m[a, 2 * r + b].astype(F32), F32)
                    w[r, rows, cols] = w[r, rows, cols] * keep.astype(BF16)
                keep = jnp.full((LANES, LANES), down_m[a, 2 * r + b].astype(F32), F32)
                dw[r, cols, rows] = dw[r, cols, rows] * keep.astype(BF16)

    mask_weights(0)
    gather_relay(0)
    gather_end(0)
    gather_start(1)

    def places(h):
        return (at_x, at_y, x, y) if h == 0 else (at_y, at_x, y, x)

    def half_of(q):
        th = q // NR
        return th, q - th * NR

    def partial_sums(q):
        th, r = half_of(q)
        tok = ab[th, :, 0].reshape(TOK, WID)
        cot = ab[th, :, 1].reshape(TOK, WID)
        slot = lax.rem(q, KEEP_OWN)
        for n in range(3):
            if n == 0:
                value = dot(tok, gw[r])
            elif n == 1:
                value = dot(tok, uw[r])
            else:
                value = dot_nt(cot, dw[r])
            for h in range(2):
                piece = value[:, h * LANES:(h + 1) * LANES].reshape(GROUP, HALF, LANES)
                own[slot, h, :, n] = piece
                part[q, h, :, n] = piece.astype(BF16)
        for h in range(2):
            at1, _, p1, _ = places(h)
            after, far, before = (lax.rem(p1 + k, SIDE) * SIDE for k in range(1, SIDE))
            for start, slot_to, sem, k in (
                (far, 0, got0, 1), (far + PAIR, 1, got0, 3),
                (after + PAIR, 2, got1, 1), (before, 3, got1, 3),
            ):
                remote(
                    part.at[q, h, pl.ds(start, PAIR)], recv1.at[q, h, slot_to],
                    send1.at[q, h], sem.at[q, h], at1(k),
                ).start()

    def add_share(q):
        slot = lax.rem(q, KEEP_OWN)
        for h in range(2):
            at1, _, p1, _ = places(h)
            drain(recv1.at[q, h, pl.ds(0, 2)], got0.at[q, h])
            after, before = (lax.rem(p1 + k, SIDE) * SIDE for k in (1, 3))
            for j, start, k in ((0, after, 1), (1, before + PAIR, 3)):
                total = own[slot, h, pl.ds(start, PAIR)] + recv1[q, h, j].astype(F32)
                chain[q, h, j] = total.astype(BF16)
                remote(
                    chain.at[q, h, j], recv1.at[q, h, 4 + j],
                    send1.at[q, h], got1.at[q, h], at1(k),
                ).start()

    def second(q):
        slot = lax.rem(q, KEEP)
        slot_own = lax.rem(q, KEEP_OWN)
        for h in range(2):
            _, at2, p1, p2 = places(h)
            drain(recv1.at[q, h, pl.ds(2, 4)], got1.at[q, h])
            for half, j in ((0, (3, 4)), (1, (2, 5))):
                total = own[slot_own, h, pl.ds(p1 * SIDE + half * PAIR, PAIR)]
                for n in j:
                    total = total + recv1[q, h, n].astype(F32)
                mid_own[slot, h, pl.ds(half * PAIR, PAIR)] = total
                mid[q, h, pl.ds(half * PAIR, PAIR)] = total.astype(BF16)
            for k in range(1, SIDE):
                to = lax.rem(p2 + k, SIDE)
                remote(
                    mid.at[q, h, to], recv2.at[q, h, k - 1],
                    send2.at[q, h], got2.at[q, h], at2(k),
                ).start()

    def activations(q):
        slot = lax.rem(q, KEEP)
        for h in range(2):
            _, at2, p1, p2 = places(h)
            drain(recv2.at[q, h], got2.at[q, h])
            total = mid_own[slot, h, p2]
            for k in range(SIDE - 1):
                total = total + recv2[q, h, k].astype(F32)
            gate, up, hidden_grad = total[0], total[1], total[2]
            sig = jax.nn.sigmoid(gate)
            act = gate * sig
            at = p1 * SIDE + p2
            full[q, h, at, 0] = (act * up).astype(BF16)
            full[q, h, at, 1] = (hidden_grad * up * sig * (1.0 + gate * (1.0 - sig))).astype(BF16)
            full[q, h, at, 2] = (hidden_grad * act).astype(BF16)
            for k in range(1, SIDE):
                block = full.at[q, h, at]
                remote(block, block, send3.at[q, h], got3.at[q, h], at2(k)).start()

    def spread(q):
        for h in range(2):
            at1, _, p1, _ = places(h)
            drain(recv2.at[q, h], got3.at[q, h])
            block = full.at[q, h, pl.ds(p1 * SIDE, SIDE)]
            for k in (1, 3):
                remote(block, block, send4.at[q, h], got4.at[q, h], at1(k)).start()

    def forward(q):
        for h in range(2):
            at1, _, p1, _ = places(h)
            drain(recv1.at[q, h, pl.ds(0, 4)], got4.at[q, h])
            after, before = (lax.rem(p1 + k, SIDE) * SIDE for k in (1, 3))
            for start, k in ((before, 1), (after + PAIR, 3)):
                block = full.at[q, h, pl.ds(start, PAIR)]
                remote(block, block, send4.at[q, h], got5.at[q, h], at1(k)).start()

    def whole(q, n):
        return jnp.concatenate(
            [full[q, h, :, n].reshape(TOK, LANES) for h in range(2)], axis=1
        )

    def finish(q):
        th, r = half_of(q)
        for h in range(2):
            drain(recv1.at[q, h, pl.ds(0, 2)], got5.at[q, h])
        hidden, gate_grad, up_grad = whole(q, 0), whole(q, 1), whole(q, 2)
        half = TOK // 2
        value = dot(hidden, dw[r])
        acc[th, 0, 0] += value[:half]
        acc[th, 1, 0] += value[half:]
        value = dot_nt(gate_grad, gw[r]) + dot_nt(up_grad, uw[r])
        acc[th, 0, 1] += value[:half]
        acc[th, 1, 1] += value[half:]

        @pl.when(q == NR - 1)
        def _():
            cores_start(0)

        @pl.when(q == NQ - 1)
        def _():
            cores_start(1)

    def weight_grads(r):
        for out, n, m in ((out_g, 1, gate_m), (out_u, 2, up_m)):
            value = dot(tok_t[0], whole(r, n)) + dot(tok_t[1], whole(r + NR, n))
            for a in range(WID // LANES):
                for b in range(2):
                    rows, cols = slice(a * LANES, (a + 1) * LANES), slice(b * LANES, (b + 1) * LANES)
                    keep = m[a, 2 * r + b].astype(F32)
                    out[r, rows, cols] = (value[rows, cols] * keep).astype(BF16)
        value = dot_tn(whole(r, 0), ab[0, :, 1].reshape(TOK, WID))
        value = value + dot_tn(whole(r + NR, 0), ab[1, :, 1].reshape(TOK, WID))
        for a in range(WID // LANES):
            for b in range(2):
                rows, cols = slice(a * LANES, (a + 1) * LANES), slice(b * LANES, (b + 1) * LANES)
                keep = down_m[a, 2 * r + b].astype(F32)
                out_d[r, cols, rows] = (value[cols, rows] * keep).astype(BF16)
        for copy in outs(r):
            copy.start()

    def outs(r):
        cols = pl.ds(pl.multiple_of(r * CH, CH), CH)
        return [
            pltpu.make_async_copy(out_g.at[r], grad_gate.at[:, cols], out_sem.at[0, r]),
            pltpu.make_async_copy(out_u.at[r], grad_up.at[:, cols], out_sem.at[1, r]),
            pltpu.make_async_copy(out_d.at[r], grad_down.at[cols, :], out_sem.at[2, r]),
        ]

    def z_buffers(th, p):
        wide = p in WIDE[th]
        return (zsend_w, zrecv_w, 1) if wide else (zsend_n, zrecv_n, 0)

    outward = ((3, 4, 1, 2, 0), (2, 0, 1, 3, 4))

    def rows_of(th, p):
        _, block, n, _ = PIECES[th][p]
        return pl.ds(block * HALF, n * HALF)

    def cores_copy(th, p):
        rows = rows_of(th, p)
        return remote(
            acc.at[th, sib, :, rows], xbuf.at[th, :, rows], x_send.at[th, p], x_recv.at[th, p], sibling
        )

    def cores_start(th):
        for p in outward[th]:
            cores_copy(th, p).start()

    def z_start(th):
        for p in outward[th]:
            cores_copy(th, p).wait_recv()
            k, rows = PIECES[th][p][0], rows_of(th, p)
            zsend, zrecv, kind = z_buffers(th, p)
            for a in range(2):
                value = acc[th, c, a, rows] + xbuf[th, a, rows]
                if k == 0:
                    zown[a] = value
                else:
                    zsend[th, a, rows] = value.astype(zsend.dtype)
            if k:
                remote(
                    zsend.at[th, :, rows], zrecv.at[th, :, rows],
                    z_send.at[th, kind], z_recv.at[th, kind], at_z(k),
                ).start()

    def z_bytes(th, sem):
        drain(zrecv_n.at[th, :, pl.ds(*ROWS_NARROW[th])], sem.at[th, 0])
        drain(zrecv_w.at[th, :, pl.ds(*ROWS_WIDE[th])], sem.at[th, 1])

    def results():
        for a, out in enumerate((layer_out, grad_tokens)):
            for half in range(2):
                value = zown[a, pl.ds(half * HALF, HALF)]
                for th in (1, 0):
                    for p, (k, block, n, start) in enumerate(PIECES[th]):
                        if k and start <= half < start + n:
                            rows = pl.ds((block + half - start) * HALF, HALF)
                            value = value + z_buffers(th, p)[1][th, a, rows].astype(F32)
                out[pl.ds(half * HALF, HALF)] = value.astype(BF16)

    @pl.loop(0, LAST)
    def _(t):
        def stage(s, work):
            @pl.when(jnp.logical_and(t >= s * LAG, t < NQ + s * LAG))
            def _():
                work(t - s * LAG)

        stage(1, add_share)
        stage(2, second)
        stage(3, activations)

        def gathered(s, work):
            j = t - WAIT - s * LAG

            @pl.when(jnp.logical_and(j >= 0, j < NQ))
            def _():
                past_early = lax.div(j + NQ - EARLY, NQ)
                past_other = lax.div(j + NQ - EARLY - NR, NQ)
                work(j + WAIT * past_early - (WAIT + NR) * past_other)

        gathered(4, spread)
        gathered(5, forward)

        @pl.when(t == NR - 1)
        def _():
            gather_relay(1)

        @pl.when(t == NR)
        def _():
            gather_end(1)

        stage(0, partial_sums)

        @pl.when(t < NR - 1)
        def _():
            mask_weights(t + 1)


        @pl.when(t == NR + 2)
        def _():
            for th in range(2):
                tok_t[th] = ab[th, :, 0].reshape(TOK, WID).T

        gathered(6, finish)
        j = t - WAIT - 6 * LAG

        @pl.when(jnp.logical_and(j >= EARLY, j < 2 * EARLY))
        def _():
            weight_grads(j - EARLY)

        @pl.when(jnp.logical_and(j >= NR + EARLY, j < NQ))
        def _():
            weight_grads(j - NR)

        @pl.when(j == NR + EARLY)
        def _():
            z_start(1)

    z_start(0)
    z_bytes(1, z_recv)
    z_bytes(0, z_recv)
    results()

    for th in range(2):
        z_bytes(th, z_send)
        for p in range(5):
            cores_copy(th, p).wait_send()
        for p, piece in enumerate(PIECES[th]):
            if piece[0]:
                z_copy(th, p).wait_send()
            to_sibling(th, p).wait_send()

    @pl.loop(0, NQ)
    def _(q):
        for h in range(2):
            drain(recv1.at[q, h], send1.at[q, h])
            drain(recv2.at[q, h], send2.at[q, h])
            drain(recv2.at[q, h], send3.at[q, h])
            drain(recv1.at[q, h], send4.at[q, h])

    @pl.loop(0, NR)
    def _(r):
        for copy in outs(r):
            copy.wait()


def hand_over(*refs):
    n = len(refs) // 2
    sem = refs[-1]
    copies = [pltpu.make_async_copy(refs[j], refs[n + j], sem.at[j]) for j in range(n)]
    for copy in copies:
        copy.start()
    for copy in copies:
        copy.wait()


def local(tokens, grad_out, gate_weight, up_weight, down_weight, gate_mask, up_mask, down_mask):
    any_spec = pl.BlockSpec(memory_space=pl.ANY)
    vmem = pl.BlockSpec(memory_space=pltpu.VMEM)
    hbm = pl.BlockSpec(memory_space=pltpu.HBM)
    dma = pltpu.SemaphoreType.DMA
    block = (3, HALF, LANES)
    shapes = [
        jax.ShapeDtypeStruct((ROWS, WID), BF16),
        jax.ShapeDtypeStruct((ROWS, WID), BF16),
        jax.ShapeDtypeStruct((WID, HID), BF16),
        jax.ShapeDtypeStruct((WID, HID), BF16),
        jax.ShapeDtypeStruct((HID, WID), BF16),
    ]
    results = pl.pallas_call(
        kernel,
        name="sparse_swiglu_step",
        out_shape=shapes,
        in_specs=[hbm] * 8,
        out_specs=[vmem, vmem, any_spec, any_spec, any_spec],
        scratch_shapes=[
            pltpu.SMEM((WID // LANES, HID // LANES), jnp.int32),
            pltpu.SMEM((WID // LANES, HID // LANES), jnp.int32),
            pltpu.SMEM((WID // LANES, HID // LANES), jnp.int32),
            pltpu.VMEM((2, 2 * ZS, 2, HALF, WID), BF16),
            pltpu.VMEM((2, WID, TOK), BF16),
            pltpu.VMEM((NR, WID, CH), BF16),
            pltpu.VMEM((NR, WID, CH), BF16),
            pltpu.VMEM((NR, CH, WID), BF16),
            pltpu.VMEM((NQ, 2, GROUP) + block, BF16),
            pltpu.VMEM((KEEP_OWN, 2, GROUP) + block, F32),
            pltpu.VMEM((NQ, 2, 6, PAIR) + block, BF16),
            pltpu.VMEM((NQ, 2, SIDE) + block, BF16),
            pltpu.VMEM((KEEP, 2, SIDE) + block, F32),
            pltpu.VMEM((NQ, 2, SIDE - 1) + block, BF16),
            pltpu.VMEM((NQ, 2, GROUP) + block, BF16),
            pltpu.VMEM((NQ, 2, 2, PAIR) + block, BF16),
            pltpu.VMEM((NR, WID, CH), BF16),
            pltpu.VMEM((NR, WID, CH), BF16),
            pltpu.VMEM((NR, CH, WID), BF16),
            pltpu.VMEM((2, 2, 2, TOK // 2, WID), F32),
            pltpu.VMEM((2, 2, TOK // 2, WID), F32),
            pltpu.VMEM((2, ROWS, WID), F32),
            pltpu.VMEM((2, 2, ZS * HALF, WID), BF16),
            pltpu.VMEM((2, 2, ZS * HALF, WID), F32),
            pltpu.VMEM((2, 2, ZS * HALF, WID), BF16),
            pltpu.VMEM((2, 2, ZS * HALF, WID), F32),
            dma((2, 2)),
            dma((3,)),
            dma((3, NR)),
            dma((2, 5)), dma((2, 5)),
            dma((2, 5)), dma((2,)),
            dma((NQ, 2)), dma((NQ, 2)), dma((NQ, 2)),
            dma((NQ, 2)), dma((NQ, 2)),
            dma((NQ, 2)), dma((NQ, 2)),
            dma((NQ, 2)), dma((NQ, 2)), dma((NQ, 2)),
            dma((3, NR)),
            dma((2, 5)), dma((2, 5)), dma((2, 2)), dma((2, 2)),
        ],
        compiler_params=pltpu.CompilerParams(
            collective_id=0, has_side_effects=True, vmem_limit_bytes=48 << 20
        ),
    )(*(
        pltpu.with_memory_space_constraint(value, pltpu.HBM)
        for value in (
            tokens, grad_out, gate_weight, up_weight, down_weight, gate_mask, up_mask, down_mask.T
        )
    ))
    return pl.pallas_call(
        hand_over,
        name="hand_over",
        out_shape=shapes,
        in_specs=[any_spec] * 5,
        out_specs=[any_spec] * 5,
        scratch_shapes=[dma((5,))],
        compiler_params=pltpu.CompilerParams(vmem_limit_bytes=1 << 20),
    )(*results)


def solution(mesh):
    wide, tall = P("inb", "outb"), P("outb", "inb")
    return jax.shard_map(
        local,
        mesh=mesh,
        in_specs=(tall, tall, wide, wide, tall, wide, wide, tall),
        out_specs=(tall, tall, wide, wide, tall),
        check_vma=False,
    )
```

```python
import functools

import jax
import jax.numpy as jnp
from jax import lax
from jax.experimental import pallas as pl
from jax.experimental.pallas import tpu as pltpu
from jax.sharding import PartitionSpec as P

MESH = pl.DeviceIdType.MESH
F32 = jnp.float32
BF16 = jnp.bfloat16
SIDE = 4
ZS = 8
GROUP = SIDE * SIDE
ROWS = 32
HALF = ROWS // 2
PAIR = SIDE // 2
TOK = GROUP * HALF
WID = 512
HID = 1792
LANES = 128
CH = 2 * LANES
NR = HID // CH
NQ = 2 * NR
LAG = 3
KEEP = LAG + 1
KEEP_OWN = 2 * LAG + 1
STAGES = 7
EARLY = 1
WAIT = NR - EARLY
LAST = NQ + WAIT + (STAGES - 1) * LAG
NEAR = ((0, 0, 2, 0), (1, 2, 2, 0), (7, 4, 2, 0), (2, 6, 1, 0), (6, 7, 1, 0))
FAR = ((3, 0, 2, 0), (5, 2, 2, 0), (4, 4, 2, 0), (2, 6, 1, 1), (6, 7, 1, 1))
PIECES = (NEAR, FAR)
WIDE = ((1, 2), (3, 4))
ROWS_WIDE = ((2 * HALF, 4 * HALF), (6 * HALF, 2 * HALF))
ROWS_NARROW = ((6 * HALF, 2 * HALF), (0, 6 * HALF))


def dot(a, b):
    return jnp.dot(a, b, preferred_element_type=F32)


def dot_nt(a, b):
    return lax.dot_general(a, b, (((1,), (1,)), ((), ())), preferred_element_type=F32)


def dot_tn(a, b):
    return lax.dot_general(a, b, (((0,), (0,)), ((), ())), preferred_element_type=F32)


def kernel(
    tokens, grad_out, gate_w, up_w, down_w, gate_mask, up_mask, down_mask,
    layer_out, grad_tokens, grad_gate, grad_up, grad_down,
    gate_m, up_m, down_m, ab, tok_t, gw, uw, dw, part, own, recv1, mid, mid_own, recv2, full,
    chain, out_g, out_u, out_d, acc, xbuf, zown, zsend_n, zsend_w, zrecv_n, zrecv_w,
    load_sem, m_sem, w_sem, a_send, a_recv, s_send, s_recv,
    send1, got0, got1, send2, got2, send3, got3, send4, got4, got5, out_sem,
    x_send, x_recv, z_send, z_recv,
):
    i = lax.axis_index("inb")
    o = lax.axis_index("outb")
    x, y = i // SIDE, lax.rem(i, SIDE)
    z, c = o // 2, lax.rem(o, 2)
    sib = 1 - c

    def at_x(k):
        return (lax.rem(x + k, SIDE) * SIDE + y, o)

    def at_y(k):
        return (x * SIDE + lax.rem(y + k, SIDE), o)

    def at_z(k):
        return (i, lax.rem(z + k, ZS) * 2 + c)

    sibling = (i, z * 2 + sib)

    def remote(src, dst, s, r, device):
        return pltpu.make_async_remote_copy(
            src_ref=src, dst_ref=dst, send_sem=s, recv_sem=r,
            device_id=device, device_id_type=MESH,
        )

    def drain(ref, sem):
        pltpu.make_async_copy(ref, ref, sem).wait()

    barrier = pltpu.get_barrier_semaphore()
    for k in range(1, SIDE):
        pl.semaphore_signal(barrier, inc=1, device_id=at_x(k), device_id_type=MESH)
        pl.semaphore_signal(barrier, inc=1, device_id=at_y(k), device_id_type=MESH)
    for k in range(1, ZS):
        pl.semaphore_signal(barrier, inc=1, device_id=at_z(k), device_id_type=MESH)
    pl.semaphore_signal(barrier, inc=1, device_id=sibling, device_id_type=MESH)

    first = []
    for half in range(2):
        rows = pl.ds(half * HALF, HALF)
        first.append(pltpu.make_async_copy(tokens.at[rows], ab.at[0, c * ZS + half, 0], load_sem.at[half, 0]))
        first.append(pltpu.make_async_copy(grad_out.at[rows], ab.at[0, c * ZS + half, 1], load_sem.at[half, 1]))
    for copy in first:
        copy.start()
    masks = [
        pltpu.make_async_copy(gate_mask, gate_m, m_sem.at[0]),
        pltpu.make_async_copy(up_mask, up_m, m_sem.at[1]),
        pltpu.make_async_copy(down_mask, down_m, m_sem.at[2]),
    ]
    for copy in masks:
        copy.start()

    def weights(r):
        cols = pl.ds(pl.multiple_of(r * CH, CH), CH)
        return [
            pltpu.make_async_copy(gate_w.at[:, cols], gw.at[r], w_sem.at[0, r]),
            pltpu.make_async_copy(up_w.at[:, cols], uw.at[r], w_sem.at[1, r]),
            pltpu.make_async_copy(down_w.at[cols, :], dw.at[r], w_sem.at[2, r]),
        ]

    @pl.loop(0, NR)
    def _(r):
        for copy in weights(r):
            copy.start()

    pl.semaphore_wait(barrier, 2 * (SIDE - 1) + ZS - 1 + 1)

    def z_copy(th, p):
        k, block, n, half = PIECES[th][p]
        return remote(
            ab.at[0, pl.ds(c * ZS + half, n)], ab.at[th, pl.ds(c * ZS + block, n)],
            a_send.at[th, p], a_recv.at[th, p], at_z(ZS - k),
        )

    def to_sibling(th, p):
        _, block, n, _ = PIECES[th][p]
        part_of = ab.at[th, pl.ds(c * ZS + block, n)]
        return remote(part_of, part_of, s_send.at[th, p], s_recv.at[th], sibling)

    def gather_start(th):
        for p in (3, 4, 2, 1, 0):
            if PIECES[th][p][0]:
                z_copy(th, p).start()
        for p, piece in enumerate(PIECES[th]):
            if not piece[0]:
                to_sibling(th, p).start()

    def gather_relay(th):
        for p, piece in enumerate(PIECES[th]):
            if piece[0]:
                z_copy(th, p).wait_recv()
                to_sibling(th, p).start()

    def gather_end(th):
        drain(ab.at[th, pl.ds(sib * ZS, ZS)], s_recv.at[th])

    for copy in first:
        copy.wait()
    gather_start(0)

    acc[...] = jnp.zeros_like(acc)
    for copy in masks:
        copy.wait()

    def mask_weights(r):
        for copy in weights(r):
            copy.wait()
        for a in range(WID // LANES):
            for b in range(2):
                rows, cols = pl.ds(a * LANES, LANES), pl.ds(b * LANES, LANES)
                for w, m in ((gw, gate_m), (uw, up_m)):
                    keep = jnp.full((LANES, LANES), m[a, 2 * r + b].astype(F32), F32)
                    w[r, rows, cols] = w[r, rows, cols] * keep.astype(BF16)
                keep = jnp.full((LANES, LANES), down_m[a, 2 * r + b].astype(F32), F32)
                dw[r, cols, rows] = dw[r, cols, rows] * keep.astype(BF16)

    mask_weights(0)
    gather_relay(0)
    gather_end(0)
    gather_start(1)

    def places(h):
        return (at_x, at_y, x, y) if h == 0 else (at_y, at_x, y, x)

    def half_of(q):
        th = q // NR
        return th, q - th * NR

    def partial_sums(q):
        th, r = half_of(q)
        tok = ab[th, :, 0].reshape(TOK, WID)
        cot = ab[th, :, 1].reshape(TOK, WID)
        slot = lax.rem(q, KEEP_OWN)
        for n in range(3):
            if n == 0:
                value = dot(tok, gw[r])
            elif n == 1:
                value = dot(tok, uw[r])
            else:
                value = dot_nt(cot, dw[r])
            for h in range(2):
                piece = value[:, h * LANES:(h + 1) * LANES].reshape(GROUP, HALF, LANES)
                own[slot, h, :, n] = piece
                part[q, h, :, n] = piece.astype(BF16)
        for h in range(2):
            at1, _, p1, _ = places(h)
            after, far, before = (lax.rem(p1 + k, SIDE) * SIDE for k in range(1, SIDE))
            for start, slot_to, sem, k in (
                (far, 0, got0, 1), (far + PAIR, 1, got0, 3),
                (after + PAIR, 2, got1, 1), (before, 3, got1, 3),
            ):
                remote(
                    part.at[q, h, pl.ds(start, PAIR)], recv1.at[q, h, slot_to],
                    send1.at[q, h], sem.at[q, h], at1(k),
                ).start()

    def add_share(q):
        slot = lax.rem(q, KEEP_OWN)
        for h in range(2):
            at1, _, p1, _ = places(h)
            drain(recv1.at[q, h, pl.ds(0, 2)], got0.at[q, h])
            after, before = (lax.rem(p1 + k, SIDE) * SIDE for k in (1, 3))
            for j, start, k in ((0, after, 1), (1, before + PAIR, 3)):
                total = own[slot, h, pl.ds(start, PAIR)] + recv1[q, h, j].astype(F32)
                chain[q, h, j] = total.astype(BF16)
                remote(
                    chain.at[q, h, j], recv1.at[q, h, 4 + j],
                    send1.at[q, h], got1.at[q, h], at1(k),
                ).start()

    def second(q):
        slot = lax.rem(q, KEEP)
        slot_own = lax.rem(q, KEEP_OWN)
        for h in range(2):
            _, at2, p1, p2 = places(h)
            drain(recv1.at[q, h, pl.ds(2, 4)], got1.at[q, h])
            for half, j in ((0, (3, 4)), (1, (2, 5))):
                total = own[slot_own, h, pl.ds(p1 * SIDE + half * PAIR, PAIR)]
                for n in j:
                    total = total + recv1[q, h, n].astype(F32)
                mid_own[slot, h, pl.ds(half * PAIR, PAIR)] = total
                mid[q, h, pl.ds(half * PAIR, PAIR)] = total.astype(BF16)
            for k in range(1, SIDE):
                to = lax.rem(p2 + k, SIDE)
                remote(
                    mid.at[q, h, to], recv2.at[q, h, k - 1],
                    send2.at[q, h], got2.at[q, h], at2(k),
                ).start()

    def activations(q):
        slot = lax.rem(q, KEEP)
        for h in range(2):
            _, at2, p1, p2 = places(h)
            drain(recv2.at[q, h], got2.at[q, h])
            total = mid_own[slot, h, p2]
            for k in range(SIDE - 1):
                total = total + recv2[q, h, k].astype(F32)
            gate, up, hidden_grad = total[0], total[1], total[2]
            sig = jax.nn.sigmoid(gate)
            act = gate * sig
            at = p1 * SIDE + p2
            full[q, h, at, 0] = (act * up).astype(BF16)
            full[q, h, at, 1] = (hidden_grad * up * sig * (1.0 + gate * (1.0 - sig))).astype(BF16)
            full[q, h, at, 2] = (hidden_grad * act).astype(BF16)
            for k in range(1, SIDE):
                block = full.at[q, h, at]
                remote(block, block, send3.at[q, h], got3.at[q, h], at2(k)).start()

    def spread(q):
        for h in range(2):
            at1, _, p1, _ = places(h)
            drain(recv2.at[q, h], got3.at[q, h])
            block = full.at[q, h, pl.ds(p1 * SIDE, SIDE)]
            for k in (1, 3):
                remote(block, block, send4.at[q, h], got4.at[q, h], at1(k)).start()

    def forward(q):
        for h in range(2):
            at1, _, p1, _ = places(h)
            drain(recv1.at[q, h, pl.ds(0, 4)], got4.at[q, h])
            after, before = (lax.rem(p1 + k, SIDE) * SIDE for k in (1, 3))
            for start, k in ((before, 1), (after + PAIR, 3)):
                block = full.at[q, h, pl.ds(start, PAIR)]
                remote(block, block, send4.at[q, h], got5.at[q, h], at1(k)).start()

    def whole(q, n):
        return jnp.concatenate(
            [full[q, h, :, n].reshape(TOK, LANES) for h in range(2)], axis=1
        )

    def finish(q):
        th, r = half_of(q)
        for h in range(2):
            drain(recv1.at[q, h, pl.ds(0, 2)], got5.at[q, h])
        hidden, gate_grad, up_grad = whole(q, 0), whole(q, 1), whole(q, 2)
        half = TOK // 2
        value = dot(hidden, dw[r])
        acc[th, 0, 0] += value[:half]
        acc[th, 1, 0] += value[half:]
        value = dot_nt(gate_grad, gw[r]) + dot_nt(up_grad, uw[r])
        acc[th, 0, 1] += value[:half]
        acc[th, 1, 1] += value[half:]

        @pl.when(q == NR - 1)
        def _():
            cores_start(0)

        @pl.when(q == NQ - 1)
        def _():
            cores_start(1)

    def weight_grads(r):
        for out, n, m in ((out_g, 1, gate_m), (out_u, 2, up_m)):
            value = dot(tok_t[0], whole(r, n)) + dot(tok_t[1], whole(r + NR, n))
            for a in range(WID // LANES):
                for b in range(2):
                    rows, cols = slice(a * LANES, (a + 1) * LANES), slice(b * LANES, (b + 1) * LANES)
                    keep = m[a, 2 * r + b].astype(F32)
                    out[r, rows, cols] = (value[rows, cols] * keep).astype(BF16)
        value = dot_tn(whole(r, 0), ab[0, :, 1].reshape(TOK, WID))
        value = value + dot_tn(whole(r + NR, 0), ab[1, :, 1].reshape(TOK, WID))
        for a in range(WID // LANES):
            for b in range(2):
                rows, cols = slice(a * LANES, (a + 1) * LANES), slice(b * LANES, (b + 1) * LANES)
                keep = down_m[a, 2 * r + b].astype(F32)
                out_d[r, cols, rows] = (value[cols, rows] * keep).astype(BF16)
        for copy in outs(r):
            copy.start()

    def outs(r):
        cols = pl.ds(pl.multiple_of(r * CH, CH), CH)
        return [
            pltpu.make_async_copy(out_g.at[r], grad_gate.at[:, cols], out_sem.at[0, r]),
            pltpu.make_async_copy(out_u.at[r], grad_up.at[:, cols], out_sem.at[1, r]),
            pltpu.make_async_copy(out_d.at[r], grad_down.at[cols, :], out_sem.at[2, r]),
        ]

    def z_buffers(th, p):
        wide = p in WIDE[th]
        return (zsend_w, zrecv_w, 1) if wide else (zsend_n, zrecv_n, 0)

    outward = ((3, 4, 1, 2, 0), (2, 0, 1, 3, 4))

    def rows_of(th, p):
        _, block, n, _ = PIECES[th][p]
        return pl.ds(block * HALF, n * HALF)

    def cores_copy(th, p):
        rows = rows_of(th, p)
        return remote(
            acc.at[th, sib, :, rows], xbuf.at[th, :, rows], x_send.at[th, p], x_recv.at[th, p], sibling
        )

    def cores_start(th):
        for p in outward[th]:
            cores_copy(th, p).start()

    def z_start(th):
        for p in outward[th]:
            cores_copy(th, p).wait_recv()
            k, rows = PIECES[th][p][0], rows_of(th, p)
            zsend, zrecv, kind = z_buffers(th, p)
            for a in range(2):
                value = acc[th, c, a, rows] + xbuf[th, a, rows]
                if k == 0:
                    zown[a] = value
                else:
                    zsend[th, a, rows] = value.astype(zsend.dtype)
            if k:
                remote(
                    zsend.at[th, :, rows], zrecv.at[th, :, rows],
                    z_send.at[th, kind], z_recv.at[th, kind], at_z(k),
                ).start()

    def z_bytes(th, sem):
        drain(zrecv_n.at[th, :, pl.ds(*ROWS_NARROW[th])], sem.at[th, 0])
        drain(zrecv_w.at[th, :, pl.ds(*ROWS_WIDE[th])], sem.at[th, 1])

    def results():
        for a, out in enumerate((layer_out, grad_tokens)):
            for half in range(2):
                value = zown[a, pl.ds(half * HALF, HALF)]
                for th in (1, 0):
                    for p, (k, block, n, start) in enumerate(PIECES[th]):
                        if k and start <= half < start + n:
                            rows = pl.ds((block + half - start) * HALF, HALF)
                            value = value + z_buffers(th, p)[1][th, a, rows].astype(F32)
                out[pl.ds(half * HALF, HALF)] = value.astype(BF16)

    @pl.loop(0, LAST)
    def _(t):
        def stage(s, work):
            @pl.when(jnp.logical_and(t >= s * LAG, t < NQ + s * LAG))
            def _():
                work(t - s * LAG)

        stage(1, add_share)
        stage(2, second)
        stage(3, activations)

        def gathered(s, work):
            j = t - WAIT - s * LAG

            @pl.when(jnp.logical_and(j >= 0, j < NQ))
            def _():
                past_early = lax.div(j + NQ - EARLY, NQ)
                past_other = lax.div(j + NQ - EARLY - NR, NQ)
                work(j + WAIT * past_early - (WAIT + NR) * past_other)

        gathered(4, spread)
        gathered(5, forward)

        @pl.when(t == NR - 1)
        def _():
            gather_relay(1)

        @pl.when(t == NR)
        def _():
            gather_end(1)

        stage(0, partial_sums)

        @pl.when(t < NR - 1)
        def _():
            mask_weights(t + 1)


        @pl.when(t == NR + 2)
        def _():
            for th in range(2):
                tok_t[th] = ab[th, :, 0].reshape(TOK, WID).T

        gathered(6, finish)
        j = t - WAIT - 6 * LAG

        @pl.when(jnp.logical_and(j >= EARLY, j < 2 * EARLY))
        def _():
            weight_grads(j - EARLY)

        @pl.when(jnp.logical_and(j >= NR + EARLY, j < NQ))
        def _():
            weight_grads(j - NR)

        @pl.when(j == NR + EARLY)
        def _():
            z_start(1)

    z_start(0)
    z_bytes(1, z_recv)
    z_bytes(0, z_recv)
    results()

    for th in range(2):
        z_bytes(th, z_send)
        for p in range(5):
            cores_copy(th, p).wait_send()
        for p, piece in enumerate(PIECES[th]):
            if piece[0]:
                z_copy(th, p).wait_send()
            to_sibling(th, p).wait_send()

    @pl.loop(0, NQ)
    def _(q):
        for h in range(2):
            drain(recv1.at[q, h], send1.at[q, h])
            drain(recv2.at[q, h], send2.at[q, h])
            drain(recv2.at[q, h], send3.at[q, h])
            drain(recv1.at[q, h], send4.at[q, h])

    @pl.loop(0, NR)
    def _(r):
        for copy in outs(r):
            copy.wait()


def hand_over(*refs):
    n = len(refs) // 2
    sem = refs[-1]
    copies = []
    for j in range(n):
        rows = refs[j].shape[0]
        step = rows if rows == ROWS else rows // 4
        for k in range(0, rows, step):
            part = pl.ds(k, step)
            copies.append(
                pltpu.make_async_copy(refs[j].at[part], refs[n + j].at[part], sem.at[len(copies)])
            )
    for copy in copies:
        copy.start()
    for copy in copies:
        copy.wait()


def local(tokens, grad_out, gate_weight, up_weight, down_weight, gate_mask, up_mask, down_mask):
    any_spec = pl.BlockSpec(memory_space=pl.ANY)
    vmem = pl.BlockSpec(memory_space=pltpu.VMEM)
    hbm = pl.BlockSpec(memory_space=pltpu.HBM)
    dma = pltpu.SemaphoreType.DMA
    block = (3, HALF, LANES)
    shapes = [
        jax.ShapeDtypeStruct((ROWS, WID), BF16),
        jax.ShapeDtypeStruct((ROWS, WID), BF16),
        jax.ShapeDtypeStruct((WID, HID), BF16),
        jax.ShapeDtypeStruct((WID, HID), BF16),
        jax.ShapeDtypeStruct((HID, WID), BF16),
    ]
    results = pl.pallas_call(
        kernel,
        name="sparse_swiglu_step",
        out_shape=shapes,
        in_specs=[hbm] * 8,
        out_specs=[vmem, vmem, any_spec, any_spec, any_spec],
        scratch_shapes=[
            pltpu.SMEM((WID // LANES, HID // LANES), jnp.int32),
            pltpu.SMEM((WID // LANES, HID // LANES), jnp.int32),
            pltpu.SMEM((WID // LANES, HID // LANES), jnp.int32),
            pltpu.VMEM((2, 2 * ZS, 2, HALF, WID), BF16),
            pltpu.VMEM((2, WID, TOK), BF16),
            pltpu.VMEM((NR, WID, CH), BF16),
            pltpu.VMEM((NR, WID, CH), BF16),
            pltpu.VMEM((NR, CH, WID), BF16),
            pltpu.VMEM((NQ, 2, GROUP) + block, BF16),
            pltpu.VMEM((KEEP_OWN, 2, GROUP) + block, F32),
            pltpu.VMEM((NQ, 2, 6, PAIR) + block, BF16),
            pltpu.VMEM((NQ, 2, SIDE) + block, BF16),
            pltpu.VMEM((KEEP, 2, SIDE) + block, F32),
            pltpu.VMEM((NQ, 2, SIDE - 1) + block, BF16),
            pltpu.VMEM((NQ, 2, GROUP) + block, BF16),
            pltpu.VMEM((NQ, 2, 2, PAIR) + block, BF16),
            pltpu.VMEM((NR, WID, CH), BF16),
            pltpu.VMEM((NR, WID, CH), BF16),
            pltpu.VMEM((NR, CH, WID), BF16),
            pltpu.VMEM((2, 2, 2, TOK // 2, WID), F32),
            pltpu.VMEM((2, 2, TOK // 2, WID), F32),
            pltpu.VMEM((2, ROWS, WID), F32),
            pltpu.VMEM((2, 2, ZS * HALF, WID), BF16),
            pltpu.VMEM((2, 2, ZS * HALF, WID), F32),
            pltpu.VMEM((2, 2, ZS * HALF, WID), BF16),
            pltpu.VMEM((2, 2, ZS * HALF, WID), F32),
            dma((2, 2)),
            dma((3,)),
            dma((3, NR)),
            dma((2, 5)), dma((2, 5)),
            dma((2, 5)), dma((2,)),
            dma((NQ, 2)), dma((NQ, 2)), dma((NQ, 2)),
            dma((NQ, 2)), dma((NQ, 2)),
            dma((NQ, 2)), dma((NQ, 2)),
            dma((NQ, 2)), dma((NQ, 2)), dma((NQ, 2)),
            dma((3, NR)),
            dma((2, 5)), dma((2, 5)), dma((2, 2)), dma((2, 2)),
        ],
        compiler_params=pltpu.CompilerParams(
            collective_id=0, has_side_effects=True, vmem_limit_bytes=48 << 20
        ),
    )(*(
        pltpu.with_memory_space_constraint(value, pltpu.HBM)
        for value in (
            tokens, grad_out, gate_weight, up_weight, down_weight, gate_mask, up_mask, down_mask.T
        )
    ))
    return pl.pallas_call(
        hand_over,
        name="hand_over",
        out_shape=shapes,
        in_specs=[any_spec] * 5,
        out_specs=[any_spec] * 5,
        scratch_shapes=[dma((14,))],
        compiler_params=pltpu.CompilerParams(vmem_limit_bytes=1 << 20),
    )(*results)


def solution(mesh):
    wide, tall = P("inb", "outb"), P("outb", "inb")
    return jax.shard_map(
        local,
        mesh=mesh,
        in_specs=(tall, tall, wide, wide, tall, wide, wide, tall),
        out_specs=(tall, tall, wide, wide, tall),
        check_vma=False,
    )
```
